32 devices in a mesh: tm: 4 (over z), query: 2 (over y), rec: 4 (over x, core).
Axes of the slice: x: 2, y: 2, z: 4, core: 2. Of those that a mesh axis runs over, the one named last changes fastest.
Arguments:
- frames: bfloat16 [4, 2048, 1024], P('rec', 'tm'), may hold values from -100 to 100
- queries: bfloat16 [4096, 1024], P('query'), may hold values from -10 to 10
- kernel: float32 [33, 4096], P(None, 'query'), may hold values from 0.01 to 0.12
- labels: int32 [4, 2048], P('rec', 'tm'), may hold values from 0 to 4095
- lengths: int32 [4], P('rec'), may hold values from 512 to 2048, as said below
Outputs:
- grad_frames: bfloat16 [4, 2048, 1024], P('rec', 'tm', 'query')
- grad_queries: bfloat16 [4096, 1024], P('query', 'rec')
- grad_kernel: float32 [33, 4096], P(None, 'query')
The draws below stay inside these ranges and needn't reach their ends.
Inputs may be any that keep to these rules, and one draw needn't show every extreme that they name: `lengths`: each entry counts the valid frames at the start of its recording; at least one recording has all 2048 frames valid.
All inputs are finite; a program needn't handle non-finite values.
Results may differ from the reference program's by a relative error of at most 0.0049.
Values sent between devices are 32-bit elements; how exact they have to be, the bound alone decides.
A program may use at most 64 MiB of HBM per device.

```python
import math
import jax
import jax.numpy as jnp
from jax import lax

W = 1024
NQ = 4096
TAPS = 33
HALF = 16
FRAMES = 2048
RECS = 4
N_QUERY = 2


def base_tables(key):
    table = jnp.clip(jax.random.normal(jax.random.fold_in(key, 11), (NQ, W), jnp.float32), -4.0, 4.0)
    blocks = jax.random.permutation(jax.random.fold_in(key, 12), N_QUERY)
    row_block = jnp.arange(NQ) // (NQ // N_QUERY)
    col_block = jnp.arange(W) // (W // N_QUERY)
    boost = jnp.where(col_block[None, :] == blocks[row_block][:, None], 2.5, 1.0)
    table = (table * boost).astype(jnp.bfloat16).astype(jnp.float32)
    kernel = jnp.exp(jax.random.uniform(jax.random.fold_in(key, 13), (TAPS, NQ), jnp.float32, math.log(0.01), math.log(0.12)))
    return (table, kernel)


def draw_queries(key, part):
    table, kernel = base_tables(key)
    return table.astype(jnp.bfloat16)


def draw_kernel(key, part):
    table, kernel = base_tables(key)
    return kernel


def draw_frames(key, part):
    noise = jnp.clip(jax.random.normal(jax.random.fold_in(key, 21), (RECS, FRAMES, W), jnp.float32), -6.0, 6.0)
    return noise.astype(jnp.bfloat16)


def draw_lengths(key, part):
    counts = jax.random.randint(jax.random.fold_in(key, 41), (RECS,), FRAMES // 4, FRAMES + 1)
    full_one = jax.random.randint(jax.random.fold_in(key, 42), (), 0, RECS)
    return jnp.where(jnp.arange(RECS) == full_one, FRAMES, counts).astype(jnp.int32)


def plant(entries, rng, smallest, largest):
    index_at = [jax.random.randint(jax.random.fold_in(rng, axis), (), 0, length) for axis, length in enumerate(entries.shape)]
    longest = entries.shape.index(max(entries.shape))
    next_to = index_at[:longest] + [(index_at[longest] + 1) % entries.shape[longest]] + index_at[longest + 1:]
    return entries.at[tuple(index_at)].set(smallest).at[tuple(next_to)].set(largest)


def setup_inputs(seed: int = 0) -> dict:
    key_list = jax.random.split(jax.random.key(seed), 6)
    frames = draw_frames(jax.random.fold_in(key_list[5], 71), 0)
    queries = draw_queries(jax.random.fold_in(key_list[5], 71), 0)
    kernel = draw_kernel(jax.random.fold_in(key_list[5], 71), 0)
    labels = plant(jax.random.randint(key_list[3], (RECS, FRAMES), 0, NQ), jax.random.fold_in(key_list[3], 1), 0, NQ - 1).astype(jnp.int32)
    lengths = draw_lengths(jax.random.fold_in(key_list[5], 71), 0)
    return {"frames": frames, "queries": queries, "kernel": kernel, "labels": labels, "lengths": lengths}


def reference(frames, queries, kernel, labels, lengths):
    logit_scale = 10.0 / math.sqrt(W)
    query_ids = jnp.arange(NQ, dtype=jnp.int32)
    frame_ids = jnp.arange(FRAMES, dtype=jnp.int32)

    def one_record(record_items):
        frame_rows, label_ids, length_now = record_items
        is_valid = frame_ids < length_now
        scores = jnp.dot(frame_rows, queries.T, preferred_element_type=jnp.float32) * logit_scale
        scores = jnp.where(is_valid[:, None], scores, 0.0)
        padded = jnp.pad(scores, ((HALF, HALF), (0, 0)))
        smooth = jnp.zeros((FRAMES, NQ), jnp.float32)
        for offset in range(TAPS):
            smooth = smooth + kernel[offset][None, :] * padded[offset:offset + FRAMES]
        softmax_out = jax.nn.softmax(smooth, axis=1)
        positive = (label_ids[:, None] == query_ids[None, :]).astype(jnp.float32)
        map_grad = jnp.where(is_valid[:, None], softmax_out - positive, 0.0)
        grad_pad = jnp.pad(map_grad, ((HALF, HALF), (0, 0)))
        score_grad = jnp.zeros((FRAMES, NQ), jnp.float32)
        for offset in range(TAPS):
            begin_row = 2 * HALF - offset
            score_grad = score_grad + kernel[offset][None, :] * grad_pad[begin_row:begin_row + FRAMES]
        score_grad = jnp.where(is_valid[:, None], score_grad, 0.0).astype(jnp.bfloat16)
        frame_grad = (jnp.dot(score_grad, queries, preferred_element_type=jnp.float32) * logit_scale).astype(jnp.bfloat16)
        query_part = lax.dot_general(score_grad, frame_rows, (((0,), (0,)), ((), ())), preferred_element_type=jnp.float32)
        kernel_part = jnp.stack([lax.optimization_barrier(jnp.sum(map_grad * padded[offset:offset + FRAMES], axis=0)) for offset in range(TAPS)])
        return (frame_grad, query_part, kernel_part)
    grad_frames, query_parts, kernel_parts = lax.map(one_record, (frames, labels, lengths))
    grad_queries = (lax.optimization_barrier(jnp.sum(query_parts, axis=0)) * logit_scale).astype(jnp.bfloat16)
    return (grad_frames, grad_queries, lax.optimization_barrier(jnp.sum(kernel_parts, axis=0)))
```

```python
import functools
import math

import jax
import jax.numpy as jnp
from jax import lax
from jax.experimental import pallas as pl
from jax.experimental.pallas import tpu as pltpu
from jax.sharding import PartitionSpec as P


GROUPS = 4
LANES = 128


def spread_taps(kern_ref, lanes):
    taps = kern_ref.shape[0]
    return [jnp.broadcast_to(kern_ref[j : j + 1, lanes], (8, LANES)) for j in range(taps)]


def tap_block(load, taps, flipped):
    count = len(taps)
    sums = [None] * GROUPS
    for o in range(8 * (GROUPS - 1) + count):
        v = load(o)
        for i in range(GROUPS):
            j = o - 8 * i
            if 0 <= j < count:
                term = taps[count - 1 - j if flipped else j] * v
                sums[i] = term if sums[i] is None else sums[i] + term
    return sums


MESH = pl.DeviceIdType.MESH


def bit_reversed(p, bits):
    return sum(((p >> k) & 1) << (bits - 1 - k) for k in range(bits))


def gradient_kernel(dims, scale, lab_hbm, len_hbm, fr_hbm, qu_hbm, kern_hbm, *refs):
    tms, peers, recs, chunk, sub, hop, tap_hop = dims
    bits = recs.bit_length() - 1
    gf_ref, gq_ref, gk_ref = refs[:3]
    scratch = refs[3:]
    acc, scratch = scratch[:bits], scratch[bits:]
    arrived, scratch = scratch[:bits], scratch[bits:]
    kacc, ksum, karrived, scratch = (scratch[0], scratch[1], scratch[2], scratch[3:])
    (mid, outer, inner, kmid, kouter, kinner, kgot, fpart, fin, sg_ref, grad) = scratch[:11]
    (sc_ref, e_ref, f_ref, lab_ref, valid_ref, xh_ref, hin, hout, stat, stat_in) = scratch[11:21]
    (fr_ref, qu_ref, kern_ref, lab_row, lab_in, len_ref) = scratch[21:27]
    scratch = scratch[27:]
    (rec_send, rec_recv, in_send, out_recv, out_send, inn_recv, f_send, f_recv) = scratch[:8]
    (h_send, h_recv, s_send, s_recv, load_sem, qu_sem) = scratch[8:14]
    (k_send, k_recv, kin_send, kout_recv, kout_send, kinn_recv, kg_send, kg_recv) = scratch[14:]

    t = lax.axis_index("tm")
    y = lax.axis_index("query")
    r = lax.axis_index("rec")
    half = tms // 2
    low = t < half
    is_end = (t == 0) | (t == tms - 1)
    is_mid = (t == half - 1) | (t == half)
    inward = jnp.where(low, t + 1, t - 1)
    outward = jnp.where(low, lax.rem(t + tms - 1, tms), lax.rem(t + 1, tms))
    my_bits = [lax.rem(r // (1 << k), 2) for k in range(bits)]
    rec_peers = [r + (1 - 2 * my_bits[k]) * (1 << k) for k in range(bits)]

    barrier = pltpu.get_barrier_semaphore()

    def greet(device):
        pl.semaphore_signal(barrier, inc=1, device_id=device, device_id_type=MESH)

    for peer in rec_peers:
        greet({"rec": peer})
    for d in range(1, peers):
        greet({"query": lax.rem(y + d, peers)})
    greet({"tm": inward})

    @pl.when(jnp.logical_not(is_end))
    def _():
        greet({"tm": outward})

    loads = [
        pltpu.make_async_copy(src, dst, load_sem.at[i])
        for i, (src, dst) in enumerate(
            ((fr_hbm, fr_ref), (lab_hbm, lab_row), (len_hbm, len_ref), (kern_hbm, kern_ref))
        )
    ]
    queries, width = qu_ref.shape
    parts = qu_sem.shape[0]
    span = queries // parts

    def qu_load(p):
        rows = pl.ds(p * span, span)
        return pltpu.make_async_copy(qu_hbm.at[rows], qu_ref.at[rows], qu_sem.at[p])

    for one in loads[:3]:
        one.start()
    for p in range(parts):
        qu_load(p).start()
    loads[3].start()

    count = queries // chunk
    subs = queries // sub
    per = chunk // sub
    rate = per // 2
    cols = width // recs
    fcols = width // peers
    row_count = sg_ref.shape[0]
    taps_n = kern_ref.shape[0]
    rim = taps_n // 2
    halo = 2 * rim
    block = 8 * GROUPS
    ext = f_ref.shape[0]
    tiles = e_ref.shape[0]
    wide = valid_ref.shape[0]
    lane = lax.broadcasted_iota(jnp.int32, (8, LANES), 1) + y * queries

    def copy(src, dst, send, recv, device):
        return pltpu.make_async_remote_copy(
            src_ref=src,
            dst_ref=dst,
            send_sem=send,
            recv_sem=recv,
            device_id=device,
            device_id_type=MESH,
        )

    def at(c):
        return pl.ds(pl.multiple_of(c * chunk, chunk), chunk)

    def sub_at(j):
        return pl.ds(pl.multiple_of(j * sub, sub), sub)

    def f_copy(d):
        p = lax.rem(y + d, peers)
        return copy(fpart.at[p], fin.at[d - 1], f_send.at[d - 1], f_recv.at[d - 1], {"query": p})

    def f_compute(p):
        tile = 128
        columns = pl.ds(pl.multiple_of(p * fcols, fcols), fcols)

        def body(i, carry):
            rows = pl.ds(pl.multiple_of(i * tile, tile), tile)
            fpart[p, rows, :] = jnp.dot(
                sg_ref[rows, :], qu_ref[:, columns], preferred_element_type=jnp.float32
            )
            return carry

        lax.fori_loop(0, row_count // tile, body, 0)

    has = [t > 0, t < tms - 1]

    def halo_copies(side):
        device = {"tm": lax.rem(t + (tms - 1 if side == 0 else 1), tms)}
        return (
            copy(
                hout.at[side],
                hin.at[1 - side],
                h_send.at[0, side],
                h_recv.at[0, 1 - side],
                device,
            ),
            copy(
                lab_row,
                lab_in.at[1 - side],
                h_send.at[1, side],
                h_recv.at[1, 1 - side],
                device,
            ),
        )

    loads[0].wait()
    for side, begin in enumerate((0, row_count - halo)):
        hout[side] = fr_ref[begin : begin + halo, :].astype(jnp.float32)
    loads[1].wait()
    pl.semaphore_wait(barrier, jnp.where(is_end, bits + peers, bits + peers + 1))

    for side in range(2):
        @pl.when(has[side])
        def _(side=side):
            for one in halo_copies(side):
                one.start()

    loads[2].wait()
    frame = lax.broadcasted_iota(jnp.int32, (wide, LANES), 0) + (t * row_count - halo)
    valid_ref[...] = jnp.where((frame >= 0) & (frame < len_ref[0]), 1.0, 0.0)
    stat[...] = jnp.zeros_like(stat)
    f_ref[...] = jnp.full_like(f_ref, -jnp.inf)

    def column_of(row):
        return jnp.transpose(jnp.broadcast_to(row.astype(jnp.float32), (LANES, LANES)))

    for i in range(row_count // LANES):
        lab_ref[rim + i * LANES : rim + (i + 1) * LANES, :] = column_of(
            lab_row[:, i * LANES : (i + 1) * LANES]
        )

    def store_scores(c, rows, part):
        for h in range(2):
            one = part[:, h * LANES : (h + 1) * LANES] * scale
            sc_ref[2 * c + h, rows, :] = jnp.where(valid_ref[rows, :] > 0, one, 0.0)

    def score(c, carry):
        rows = pl.ds(pl.multiple_of(c * 2 * LANES, 2 * LANES), 2 * LANES)
        part = lax.dot_general(
            fr_ref[...],
            qu_ref[rows, :],
            (((1,), (1,)), ((), ())),
            preferred_element_type=jnp.float32,
        )
        store_scores(c, slice(halo, halo + row_count), part)
        return carry

    each = tiles // 2 // parts
    for p in range(parts):
        qu_load(p).wait()
        lax.fori_loop(p * each, (p + 1) * each, score, 0)

    for side in range(2):
        @pl.when(has[side])
        def _(side=side):
            for one in halo_copies(1 - side):
                one.wait_recv()

        @pl.when(jnp.logical_not(has[side]))
        def _(side=side):
            hin[side] = jnp.zeros((halo, width), jnp.float32)
            lab_in[side] = jnp.zeros((1, row_count), jnp.int32)

    xh_ref[:halo, :] = hin[0].astype(jnp.bfloat16)
    xh_ref[halo:, :] = hin[1].astype(jnp.bfloat16)
    lab_ref[:rim, :] = column_of(lab_in[0, :, row_count - LANES :])[LANES - rim :, :]
    lab_ref[rim + row_count :, :] = column_of(lab_in[1, :, :LANES])[:rim, :]

    def halo_score(c, carry):
        rows = pl.ds(pl.multiple_of(c * 2 * LANES, 2 * LANES), 2 * LANES)
        part = lax.dot_general(
            xh_ref[...],
            qu_ref[rows, :],
            (((1,), (1,)), ((), ())),
            preferred_element_type=jnp.float32,
        )
        store_scores(c, slice(0, halo), part[:halo])
        store_scores(c, slice(halo + row_count, wide), part[halo:])
        return carry

    lax.fori_loop(0, tiles // 2, halo_score, 0)
    loads[3].wait()

    def smoothed(c, carry):
        taps = spread_taps(kern_ref, at(c))

        def body(g, carry):
            base = pl.multiple_of(g * block, block)
            sums = tap_block(lambda o: sc_ref[c, pl.ds(base + o, 8), :], taps, False)
            for i in range(GROUPS):
                rows = pl.ds(base + 8 * i, 8)
                e_ref[c, rows, :] = sums[i]
                f_ref[rows, :] = jnp.maximum(f_ref[rows, :], sums[i])
            return carry

        return lax.fori_loop(0, ext // block, body, carry)

    lax.fori_loop(0, tiles, smoothed, 0)

    diagonal = lax.broadcasted_iota(jnp.int32, (block, LANES), 0) == lax.broadcasted_iota(
        jnp.int32, (block, LANES), 1
    )

    def finish(g, carry):
        rows = pl.ds(pl.multiple_of(g * block, block), block)
        top = jnp.max(f_ref[rows, :], axis=1, keepdims=True)
        top = jnp.broadcast_to(top, (block, LANES))
        total = jnp.zeros((block, LANES), jnp.float32)
        for c in range(tiles):
            e = jnp.exp(e_ref[c, rows, :] - top)
            e_ref[c, rows, :] = e
            total = total + e
        total = jnp.broadcast_to(jnp.sum(total, axis=1, keepdims=True), (block, LANES))
        for i, value in enumerate((top, total)):
            picked = jnp.where(diagonal, value, 0.0)
            stat[0, i, pl.ds(g, 1), :] = jnp.sum(picked, axis=0, keepdims=True)
        return carry

    lax.fori_loop(0, ext // block, finish, 0)

    def stat_copy(k):
        bit = lax.rem(y // (1 << k), 2)
        device = {"query": y + (1 - 2 * bit) * (1 << k)}
        return copy(stat.at[k], stat_in.at[k], s_send.at[k], s_recv.at[k], device)

    rounds = peers.bit_length() - 1
    for k in range(rounds):
        stat_copy(k).start()
        stat_copy(k).wait_recv()
        top = jnp.maximum(stat[k, 0], stat_in[k, 0])
        stat[k + 1, 0] = top
        stat[k + 1, 1] = stat[k, 1] * jnp.exp(stat[k, 0] - top) + stat_in[k, 1] * jnp.exp(
            stat_in[k, 0] - top
        )
    stat[rounds, 1] = jnp.exp(stat[0, 0] - stat[rounds, 0]) / stat[rounds, 1]

    def widen(g, carry):
        rows = pl.ds(pl.multiple_of(g * block, block), block)
        row = jnp.broadcast_to(stat[rounds, 1, pl.ds(g, 1), :], (block, LANES))
        factor = jnp.sum(jnp.where(diagonal, row, 0.0), axis=1, keepdims=True)
        factor = jnp.broadcast_to(factor, (block, LANES))
        valid = valid_ref[pl.ds(pl.multiple_of(g * block, block) + rim, block), :] > 0
        f_ref[rows, :] = jnp.where(valid, factor, -1.0)
        return carry

    lax.fori_loop(0, ext // block, widen, 0)

    def map_gradient(c):
        first = (lane + c * chunk).astype(jnp.float32)

        def body(g, carry):
            for i in range(GROUPS):
                rows = pl.ds(pl.multiple_of(g * block + 8 * i, 8), 8)
                hit = jnp.where(lab_ref[rows, :] == first, 1.0, 0.0)
                factor = f_ref[rows, :]
                value = e_ref[c, rows, :] * jnp.maximum(factor, 0.0) - hit
                grad[c, rows, :] = jnp.where(factor >= 0.0, value, 0.0)
            return carry

        lax.fori_loop(0, ext // block, body, 0)

    def score_gradient(c):
        taps = spread_taps(kern_ref, at(c))

        def body(g, carry):
            base = pl.multiple_of(g * block, block)
            sums = tap_block(lambda o: grad[c, pl.ds(base + o, 8), :], taps, True)
            valid = f_ref[pl.ds(base + rim, block), :] >= 0.0
            total = jnp.where(valid, jnp.concatenate(sums, axis=0), 0.0)
            sg_ref[pl.ds(base, block), at(c)] = total.astype(jnp.bfloat16)
            return carry

        lax.fori_loop(0, row_count // block, body, 0)

    def tap_gradient(c):
        def body(g, sums):
            base = pl.multiple_of(g * block, block)
            held = [grad[c, pl.ds(base + rim + 8 * i, 8), :] for i in range(GROUPS)]
            sums = list(sums)
            for o in range(8 * (GROUPS - 1) + taps_n):
                v = sc_ref[c, pl.ds(base + rim + o, 8), :]
                for i in range(GROUPS):
                    j = o - 8 * i
                    if 0 <= j < taps_n:
                        sums[j] = sums[j] + held[i] * v
            return tuple(sums)

        zero = jnp.zeros((8, LANES), jnp.float32)
        sums = lax.fori_loop(0, row_count // block, body, (zero,) * taps_n)
        for j in range(taps_n):
            kacc[c, j : j + 1, :] = jnp.sum(sums[j], axis=0, keepdims=True)

    def rec_copy(k, j):
        n = recs >> k
        theirs = (1 - my_bits[k]) * (n // 2)
        return copy(
            acc[k].at[pl.ds(theirs, n // 2), sub_at(j)],
            arrived[k].at[:, sub_at(j)],
            rec_send.at[k, j],
            rec_recv.at[k, j],
            {"rec": rec_peers[k]},
        )

    def summed(k, j):
        rec_copy(k, j).wait_recv()
        n = recs >> k
        mine = my_bits[k] * (n // 2)
        return acc[k][pl.ds(mine, n // 2), sub_at(j), :] + arrived[k][:, sub_at(j), :]

    def inward_copy(j, to_mid):
        big = inner if to_mid else outer
        recv = inn_recv if to_mid else out_recv
        return copy(mid.at[sub_at(j)], big.at[sub_at(j)], in_send.at[j], recv.at[j], {"tm": inward})

    def outward_copy(j):
        return copy(
            inner.at[sub_at(j)],
            inner.at[sub_at(j)],
            out_send.at[j],
            inn_recv.at[j],
            {"tm": outward},
        )

    def produce(c):
        map_gradient(c)
        score_gradient(c)
        part = lax.dot_general(
            sg_ref[:, at(c)],
            fr_ref[...],
            (((0,), (0,)), ((), ())),
            preferred_element_type=jnp.float32,
        )
        for p in range(recs):
            j = bit_reversed(p, bits)
            acc[0][p, at(c), :] = part[:, j * cols : (j + 1) * cols]
        for h in range(per):
            rec_copy(0, c * per + h).start()

    def exchange(k, j):
        acc[k][:, sub_at(j), :] = summed(k - 1, j)
        rec_copy(k, j).start()

    def gather_in(j):
        mid[sub_at(j), :] = summed(bits - 1, j)[0]

        @pl.when(jnp.logical_not(is_end))
        def _():
            inward_copy(j, False).wait_recv()
            mid[sub_at(j), :] += outer[sub_at(j), :]

        @pl.when(is_mid)
        def _():
            inward_copy(j, True).start()

        @pl.when(jnp.logical_not(is_mid))
        def _():
            inward_copy(j, False).start()

    def spread_out(j):
        inward_copy(j, True).wait_recv()

        @pl.when(is_mid)
        def _():
            inner[sub_at(j), :] += mid[sub_at(j), :]

        @pl.when(jnp.logical_not(is_end))
        def _():
            outward_copy(j).start()

        gq_ref[sub_at(j), :] = (inner[sub_at(j), :] * scale).astype(gq_ref.dtype)
        for k in range(bits):
            rec_copy(k, j).wait_send()
        inward_copy(j, False).wait_send()

    def k_copy(k, i):
        src = kacc.at[2 * i + 1 - my_bits[0]] if k == 0 else ksum.at[k - 1, i]
        return copy(src, karrived.at[k, i], k_send.at[k, i], k_recv.at[k, i], {"rec": rec_peers[k]})

    def k_summed(k, i):
        k_copy(k, i).wait_recv()
        own = kacc[2 * i + my_bits[0]] if k == 0 else ksum[k - 1, i]
        return own + karrived[k, i]

    def k_inward(i, to_mid):
        dst = kinner if to_mid else kouter
        recv = kinn_recv if to_mid else kout_recv
        return copy(kmid.at[i], dst.at[i], kin_send.at[i], recv.at[i], {"tm": inward})

    def k_outward(i):
        return copy(kinner.at[i], kinner.at[i], kout_send.at[i], kinn_recv.at[i], {"tm": outward})

    def k_give(i):
        return copy(kinner.at[i], kgot.at[i], kg_send.at[i], kg_recv.at[i], {"rec": rec_peers[0]})

    def k_exchange(k, i):
        ksum[k - 1, i] = k_summed(k - 1, i)
        k_copy(k, i).start()

    def k_gather(i):
        kmid[i] = k_summed(bits - 1, i)

        @pl.when(jnp.logical_not(is_end))
        def _():
            k_inward(i, False).wait_recv()
            kmid[i] += kouter[i]

        @pl.when(is_mid)
        def _():
            k_inward(i, True).start()

        @pl.when(jnp.logical_not(is_mid))
        def _():
            k_inward(i, False).start()

    def k_spread(i):
        k_inward(i, True).wait_recv()

        @pl.when(is_mid)
        def _():
            kinner[i] += kmid[i]

        k_give(i).start()

        @pl.when(jnp.logical_not(is_end))
        def _():
            k_outward(i).start()

        gk_ref[:, at(2 * i + my_bits[0])] = kinner[i]
        for k in range(bits):
            k_copy(k, i).wait_send()
        k_inward(i, False).wait_send()

    def k_take(i):
        k_give(i).wait_recv()
        gk_ref[:, at(2 * i + 1 - my_bits[0])] = kgot[i]

    reach = half - 1
    away = jnp.where(low, reach - t, t - half)

    def plan(step, first, spread, gather, swap, take):
        base = first + (bits - 1) * step
        ends = base + 2 * step * reach + step
        late = [(ends + first, take)] if take else []
        late += [(base + step * (reach + away + 1), spread), (base + step * (reach - away), gather)]
        late += [
            (first + (k - 1) * step, functools.partial(swap, k)) for k in range(bits - 1, 0, -1)
        ]
        return late, ends + (first if take else 0)

    stages, last = plan(hop, rate, spread_out, gather_in, exchange, None)
    k_stages, k_last = plan(tap_hop, 1, k_spread, k_gather, k_exchange, k_take)
    begun = 2 * count
    steps = begun + max((last + rate - 1) // rate, k_last)

    def step(s, carry):
        @pl.when(s < count)
        def _():
            produce(s)

        @pl.when(s == count)
        def _():
            for d in range(1, peers):
                f_compute(lax.rem(y + d, peers))
                f_copy(d).start()

        @pl.when(s == begun)
        def _():
            f_compute(y)

        c = s - count

        @pl.when((c >= 0) & (c < count))
        def _():
            tap_gradient(c)

            @pl.when(lax.rem(c, 2) == 1)
            def _():
                k_copy(0, c // 2).start()

        for i in range(rate):
            for delay, stage in stages:
                tick = s * rate + i - delay

                @pl.when((tick >= 0) & (tick < subs))
                def _(stage=stage, tick=tick):
                    stage(tick)

        for delay, stage in k_stages:
            tick = c - delay

            @pl.when((tick >= 0) & (tick < count) & (lax.rem(tick + 2, 2) == 1))
            def _(stage=stage, tick=tick):
                stage(tick // 2)

        return carry

    lax.fori_loop(0, steps, step, 0)

    for d in range(1, peers):
        f_copy(d).wait_recv()
    total = fpart[y]
    for d in range(1, peers):
        total = total + fin[d - 1]
    gf_ref[...] = (total * scale).astype(gf_ref.dtype)
    for d in range(1, peers):
        f_copy(d).wait_send()

    @pl.when(jnp.logical_not(is_end))
    def _():
        def drain(j, carry):
            outward_copy(j).wait_send()
            return carry

        lax.fori_loop(0, subs, drain, 0)

    def k_drain(i, carry):
        k_give(i).wait_send()

        @pl.when(jnp.logical_not(is_end))
        def _():
            k_outward(i).wait_send()

        return carry

    lax.fori_loop(0, count // 2, k_drain, 0)
    for k in range(rounds):
        stat_copy(k).wait_send()
    for side in range(2):
        @pl.when(has[side])
        def _(side=side):
            for one in halo_copies(side):
                one.wait_send()


SPLIT = 2
HOP = 3
TAP_HOP = 2
PARTS = 2


def gradients(labels, lengths, frame_rows, queries, kernel, scale):
    tms, peers, recs = (lax.axis_size("tm"), lax.axis_size("query"), lax.axis_size("rec"))
    bits = recs.bit_length() - 1
    row_count, width = frame_rows.shape
    query_count = queries.shape[0]
    taps = kernel.shape[0]
    chunk = LANES
    sub = chunk // SPLIT
    count = query_count // chunk
    subs = query_count // sub
    cols, fcols = (width // recs, width // peers)
    rim = taps // 2
    ext, wide = (row_count + 2 * rim, row_count + 4 * rim)
    rounds = peers.bit_length() - 1
    stat_rows = (ext // (8 * GROUPS) + 7) // 8 * 8
    pairs = count // 2
    f32 = jnp.float32
    vmem = pltpu.VMEM
    small = vmem((pairs, taps, chunk), f32)
    block = vmem((query_count, cols), f32)
    scratch = [vmem((recs >> k, query_count, cols), f32) for k in range(bits)]
    scratch += [vmem((recs >> (k + 1), query_count, cols), f32) for k in range(bits)]
    scratch += [
        vmem((count, taps, chunk), f32),
        vmem((max(bits - 1, 1), pairs, taps, chunk), f32),
        vmem((bits, pairs, taps, chunk), f32),
    ]
    scratch += [block] * 3 + [small] * 4
    scratch += [
        vmem((peers, row_count, fcols), f32),
        vmem((peers - 1, row_count, fcols), f32),
        vmem((row_count, query_count), jnp.bfloat16),
        vmem((count, ext, chunk), f32),
        vmem((count, wide, chunk), f32),
        vmem((count, ext, chunk), f32),
        vmem((ext, chunk), f32),
        vmem((ext, chunk), f32),
        vmem((wide, chunk), f32),
        vmem((4 * rim, width), jnp.bfloat16),
        vmem((2, 2 * rim, width), f32),
        vmem((2, 2 * rim, width), f32),
        vmem((rounds + 1, 2, stat_rows, LANES), f32),
        vmem((rounds, 2, stat_rows, LANES), f32),
        vmem((row_count, width), jnp.bfloat16),
        vmem((query_count, width), jnp.bfloat16),
        vmem((taps, query_count), f32),
        vmem((1, row_count), jnp.int32),
        vmem((2, 1, row_count), jnp.int32),
        pltpu.SMEM((1,), jnp.int32),
    ]
    dma = pltpu.SemaphoreType.DMA
    scratch += [dma((bits, subs))] * 2 + [dma((subs,))] * 4 + [dma((peers - 1,))] * 2
    scratch += [dma((2, 2))] * 2 + [dma((rounds,))] * 2 + [dma((4,)), dma((PARTS,))]
    scratch += [dma((bits, pairs))] * 2 + [dma((pairs,))] * 6
    hbm = pl.BlockSpec(memory_space=pl.ANY)
    dims = (tms, peers, recs, chunk, sub, HOP, TAP_HOP)
    return pl.pallas_call(
        functools.partial(gradient_kernel, dims, scale),
        out_shape=(
            pltpu.VMEM((row_count, fcols), jnp.bfloat16),
            pltpu.VMEM((query_count, cols), jnp.bfloat16),
            pltpu.VMEM((taps, query_count), f32),
        ),
        in_specs=[hbm] * 5,
        out_specs=(pl.BlockSpec(memory_space=pltpu.VMEM),) * 3,
        scratch_shapes=scratch,
        compiler_params=pltpu.CompilerParams(
            collective_id=0, has_side_effects=True, vmem_limit_bytes=60 * 1024 * 1024
        ),
        name="gradients",
    )(labels, lengths, frame_rows, queries, kernel)


def store_kernel(*refs):
    ins, outs, sem = refs[:3], refs[3:6], refs[6]
    copies = [pltpu.make_async_copy(a, b, sem.at[i]) for i, (a, b) in enumerate(zip(ins, outs))]
    for one in copies:
        one.start()
    for one in copies:
        one.wait()


def store(arrays):
    return pl.pallas_call(
        store_kernel,
        out_shape=tuple(jax.ShapeDtypeStruct(a.shape, a.dtype) for a in arrays),
        in_specs=[pl.BlockSpec(memory_space=pltpu.VMEM)] * 3,
        out_specs=(pl.BlockSpec(memory_space=pl.ANY),) * 3,
        scratch_shapes=[pltpu.SemaphoreType.DMA((3,))],
        compiler_params=pltpu.CompilerParams(vmem_limit_bytes=4 * 1024 * 1024),
        name="store",
    )(*arrays)


def per_device(frames, queries, kernel, labels, lengths):
    frame_rows = frames[0]
    width = frame_rows.shape[1]
    logit_scale = 10.0 / math.sqrt(width)
    grad_frames, grad_queries, grad_kernel = store(
        gradients(labels, lengths, frame_rows, queries, kernel, logit_scale)
    )
    return (grad_frames[None], grad_queries, grad_kernel)


def solution(mesh):
    in_specs = (P("rec", "tm", None), P("query", None), P(None, "query"), P("rec", "tm"), P("rec"))
    out_specs = (P("rec", "tm", "query"), P("query", "rec"), P(None, "query"))
    return jax.shard_map(
        per_device, mesh=mesh, in_specs=in_specs, out_specs=out_specs, check_vma=False
    )
```

```python
import functools
import math

import jax
import jax.numpy as jnp
from jax import lax
from jax.experimental import pallas as pl
from jax.experimental.pallas import tpu as pltpu
from jax.sharding import PartitionSpec as P


GROUPS = 4
LANES = 128


def spread_taps(kern_ref, lanes):
    taps = kern_ref.shape[0]
    return [jnp.broadcast_to(kern_ref[j : j + 1, lanes], (8, LANES)) for j in range(taps)]


SPAN = 4
AHEAD = 3


def plus(a, b):
    return [x + b[i] if i < len(b) else x for i, x in enumerate(a)]


def minus(a):
    return [-x for x in a]


def spread_filters(filt_ref, h):
    even, odd = h[0::2], h[1::2]
    both = plus(even, odd)
    filters = (
        plus(both[0::2], both[1::2]),
        both[0::2],
        minus(both[1::2]),
        plus(even[0::2], even[1::2]),
        even[0::2],
        minus(even[1::2]),
        minus(plus(odd[0::2], odd[1::2])),
        minus(odd[0::2]),
        odd[1::2],
    )
    depth = len(filters[0])
    for n, one in enumerate(filters):
        for i, x in enumerate(one):
            filt_ref[n * depth + i] = x
    return [len(one) for one in filters]


def spread_streams(load, strm_ref, groups):
    def one_group(g):
        x = [load(pl.multiple_of(g * 32, 32) + o) for o in range(7)]
        e = [x[o] - x[o + 2] for o in range(5)]
        f = [e[o] - e[o + 1] for o in range(4)]
        rows = pl.ds(pl.multiple_of(g * 8, 8), 8)
        streams = (x[3], e[1], e[3], x[2] - x[3], f[0], f[2], x[3] - x[4], f[1], f[3])
        for n, one in enumerate(streams):
            strm_ref[n, rows, :] = one

    def body(i, carry):
        for k in range(AHEAD):
            one_group(i * AHEAD + k)
        return carry

    lax.fori_loop(0, groups // AHEAD, body, 0)
    for g in range(groups // AHEAD * AHEAD, groups):
        one_group(g)


def fir(strm_ref, filt_ref, lengths, base, span):
    depth = lengths[0]
    done = []
    for n, count in enumerate(lengths):
        taps = [filt_ref[n * depth + i] for i in range(count)]
        sums = list(done[n // 3 * 3]) if n % 3 else [None] * span
        for o in range(8 * (span - 1) + count):
            v = strm_ref[n, pl.ds(base + o, 8), :]
            for k in range(span):
                i = o - 8 * k
                if 0 <= i < count:
                    term = taps[i] * v
                    sums[k] = term if sums[k] is None else sums[k] + term
        done.append(sums)
    add = lambda a, b: [x + z for x, z in zip(a, b)]
    return (
        add(done[1], done[4]),
        add(done[1], done[7]),
        add(done[2], done[5]),
        add(done[2], done[8]),
    )


MESH = pl.DeviceIdType.MESH


def bit_reversed(p, bits):
    return sum(((p >> k) & 1) << (bits - 1 - k) for k in range(bits))


def gradient_kernel(dims, scale, lab_hbm, len_hbm, fr_hbm, qu_hbm, kern_hbm, *refs):
    tms, peers, recs, chunk, sub, hop, tap_hop = dims
    bits = recs.bit_length() - 1
    gf_ref, gq_ref, gk_ref = refs[:3]
    scratch = refs[3:]
    acc, scratch = scratch[:bits], scratch[bits:]
    arrived, scratch = scratch[:bits], scratch[bits:]
    kacc, ksum, karrived, scratch = (scratch[0], scratch[1], scratch[2], scratch[3:])
    (mid, outer, inner, kmid, kouter, kinner, kgot, fpart, fin, sg_ref, grad) = scratch[:11]
    (sc_ref, e_ref, f_ref, lab_ref, valid_ref, xh_ref, hin, hout, stat, stat_in) = scratch[11:21]
    (fr_ref, qu_ref, kern_ref, lab_row, lab_in, len_ref, strm_ref, filt_ref, turn) = scratch[21:30]
    scratch = scratch[30:]
    (rec_send, rec_recv, in_send, out_recv, out_send, inn_recv, f_send, f_recv) = scratch[:8]
    (h_send, h_recv, s_send, s_recv, load_sem, qu_sem) = scratch[8:14]
    (k_send, k_recv, kin_send, kout_recv, kout_send, kinn_recv, kg_send, kg_recv) = scratch[14:]

    t = lax.axis_index("tm")
    y = lax.axis_index("query")
    r = lax.axis_index("rec")
    half = tms // 2
    low = t < half
    is_end = (t == 0) | (t == tms - 1)
    is_mid = (t == half - 1) | (t == half)
    inward = jnp.where(low, t + 1, t - 1)
    outward = jnp.where(low, lax.rem(t + tms - 1, tms), lax.rem(t + 1, tms))
    my_bits = [lax.rem(r // (1 << k), 2) for k in range(bits)]
    rec_peers = [r + (1 - 2 * my_bits[k]) * (1 << k) for k in range(bits)]

    barrier = pltpu.get_barrier_semaphore()

    def greet(device):
        pl.semaphore_signal(barrier, inc=1, device_id=device, device_id_type=MESH)

    for peer in rec_peers:
        greet({"rec": peer})
    for d in range(1, peers):
        greet({"query": lax.rem(y + d, peers)})
    greet({"tm": inward})

    @pl.when(jnp.logical_not(is_end))
    def _():
        greet({"tm": outward})

    loads = [
        pltpu.make_async_copy(src, dst, load_sem.at[i])
        for i, (src, dst) in enumerate(
            ((fr_hbm, fr_ref), (lab_hbm, lab_row), (len_hbm, len_ref), (kern_hbm, kern_ref))
        )
    ]
    queries, width = qu_ref.shape
    parts = qu_sem.shape[0]
    span = queries // parts

    def qu_load(p):
        rows = pl.ds(p * span, span)
        return pltpu.make_async_copy(qu_hbm.at[rows], qu_ref.at[rows], qu_sem.at[p])

    for one in loads[:3]:
        one.start()
    for p in range(parts):
        qu_load(p).start()
    loads[3].start()

    count = queries // chunk
    subs = queries // sub
    per = chunk // sub
    rate = per // 2
    cols = width // recs
    fcols = width // peers
    row_count = sg_ref.shape[0]
    taps_n = kern_ref.shape[0]
    rim = taps_n // 2
    halo = 2 * rim
    block = 8 * GROUPS
    ext = f_ref.shape[0]
    tiles = e_ref.shape[0]
    wide = valid_ref.shape[0]
    lane = lax.broadcasted_iota(jnp.int32, (8, LANES), 1) + y * queries

    def copy(src, dst, send, recv, device):
        return pltpu.make_async_remote_copy(
            src_ref=src,
            dst_ref=dst,
            send_sem=send,
            recv_sem=recv,
            device_id=device,
            device_id_type=MESH,
        )

    def at(c):
        return pl.ds(pl.multiple_of(c * chunk, chunk), chunk)

    def sub_at(j):
        return pl.ds(pl.multiple_of(j * sub, sub), sub)

    def f_copy(d):
        p = lax.rem(y + d, peers)
        return copy(fpart.at[p], fin.at[d - 1], f_send.at[d - 1], f_recv.at[d - 1], {"query": p})

    def f_compute(p):
        tile = 128
        columns = pl.ds(pl.multiple_of(p * fcols, fcols), fcols)

        def body(i, carry):
            rows = pl.ds(pl.multiple_of(i * tile, tile), tile)
            fpart[p, rows, :] = jnp.dot(
                sg_ref[rows, :], qu_ref[:, columns], preferred_element_type=jnp.float32
            )
            return carry

        lax.fori_loop(0, row_count // tile, body, 0)

    has = [t > 0, t < tms - 1]

    def halo_copies(side):
        device = {"tm": lax.rem(t + (tms - 1 if side == 0 else 1), tms)}
        return (
            copy(
                hout.at[side],
                hin.at[1 - side],
                h_send.at[0, side],
                h_recv.at[0, 1 - side],
                device,
            ),
            copy(
                lab_row,
                lab_in.at[1 - side],
                h_send.at[1, side],
                h_recv.at[1, 1 - side],
                device,
            ),
        )

    loads[0].wait()
    for side, begin in enumerate((0, row_count - halo)):
        hout[side] = fr_ref[begin : begin + halo, :].astype(jnp.float32)
    loads[1].wait()
    pl.semaphore_wait(barrier, jnp.where(is_end, bits + peers, bits + peers + 1))

    for side in range(2):
        @pl.when(has[side])
        def _(side=side):
            for one in halo_copies(side):
                one.start()

    loads[2].wait()
    frame = lax.broadcasted_iota(jnp.int32, (wide, LANES), 0) + (t * row_count - halo)
    valid_ref[...] = jnp.where((frame >= 0) & (frame < len_ref[0]), 1.0, 0.0)
    stat[...] = jnp.zeros_like(stat)
    f_ref[...] = jnp.full_like(f_ref, -jnp.inf)

    def column_of(row):
        return jnp.transpose(jnp.broadcast_to(row.astype(jnp.float32), (LANES, LANES)))

    for i in range(row_count // LANES):
        lab_ref[rim + i * LANES : rim + (i + 1) * LANES, :] = column_of(
            lab_row[:, i * LANES : (i + 1) * LANES]
        )

    def store_scores(c, rows, part):
        for h in range(2):
            one = part[:, h * LANES : (h + 1) * LANES] * scale
            sc_ref[2 * c + h, rows, :] = jnp.where(valid_ref[rows, :] > 0, one, 0.0)

    def score(c, carry):
        rows = pl.ds(pl.multiple_of(c * 2 * LANES, 2 * LANES), 2 * LANES)
        part = lax.dot_general(
            fr_ref[...],
            qu_ref[rows, :],
            (((1,), (1,)), ((), ())),
            preferred_element_type=jnp.float32,
        )
        store_scores(c, slice(halo, halo + row_count), part)
        return carry

    each = tiles // 2 // parts
    for p in range(parts):
        qu_load(p).wait()
        lax.fori_loop(p * each, (p + 1) * each, score, 0)

    for side in range(2):
        @pl.when(has[side])
        def _(side=side):
            for one in halo_copies(1 - side):
                one.wait_recv()

        @pl.when(jnp.logical_not(has[side]))
        def _(side=side):
            hin[side] = jnp.zeros((halo, width), jnp.float32)
            lab_in[side] = jnp.zeros((1, row_count), jnp.int32)

    xh_ref[:halo, :] = hin[0].astype(jnp.bfloat16)
    xh_ref[halo:, :] = hin[1].astype(jnp.bfloat16)
    lab_ref[:rim, :] = column_of(lab_in[0, :, row_count - LANES :])[LANES - rim :, :]
    lab_ref[rim + row_count :, :] = column_of(lab_in[1, :, :LANES])[:rim, :]

    def halo_score(c, carry):
        rows = pl.ds(pl.multiple_of(c * 2 * LANES, 2 * LANES), 2 * LANES)
        part = lax.dot_general(
            xh_ref[...],
            qu_ref[rows, :],
            (((1,), (1,)), ((), ())),
            preferred_element_type=jnp.float32,
        )
        store_scores(c, slice(0, halo), part[:halo])
        store_scores(c, slice(halo + row_count, wide), part[halo:])
        return carry

    lax.fori_loop(0, tiles // 2, halo_score, 0)
    loads[3].wait()

    def smoothed(c, carry):
        lengths = spread_filters(filt_ref, spread_taps(kern_ref, at(c)))
        spread_streams(lambda o: sc_ref[c, pl.ds(o, 8, stride=4), :], strm_ref, wide // 32)

        def piece(base, span):
            for p, sums in enumerate(fir(strm_ref, filt_ref, lengths, base, span)):
                for k in range(span):
                    rows = pl.ds(4 * base + 32 * k + p, 8, stride=4)
                    e_ref[c, rows, :] = sums[k]
                    f_ref[rows, :] = jnp.maximum(f_ref[rows, :], sums[k])

        def body(g, carry):
            piece(pl.multiple_of(g * 8 * SPAN, 8), SPAN)
            return carry

        whole = ext // (32 * SPAN)
        lax.fori_loop(0, whole, body, 0)
        for g in range(whole * SPAN, ext // 32):
            piece(8 * g, 1)
        return carry

    lax.fori_loop(0, tiles, smoothed, 0)

    diagonal = lax.broadcasted_iota(jnp.int32, (block, LANES), 0) == lax.broadcasted_iota(
        jnp.int32, (block, LANES), 1
    )

    def finish(g, carry):
        rows = pl.ds(pl.multiple_of(g * block, block), block)
        top = jnp.max(f_ref[rows, :], axis=1, keepdims=True)
        top = jnp.broadcast_to(top, (block, LANES))
        total = jnp.zeros((block, LANES), jnp.float32)
        for c in range(tiles):
            e = jnp.exp(e_ref[c, rows, :] - top)
            e_ref[c, rows, :] = e
            total = total + e
        total = jnp.broadcast_to(jnp.sum(total, axis=1, keepdims=True), (block, LANES))
        for i, value in enumerate((top, total)):
            picked = jnp.where(diagonal, value, 0.0)
            stat[0, i, pl.ds(g, 1), :] = jnp.sum(picked, axis=0, keepdims=True)
        return carry

    lax.fori_loop(0, ext // block, finish, 0)

    def stat_copy(k):
        bit = lax.rem(y // (1 << k), 2)
        device = {"query": y + (1 - 2 * bit) * (1 << k)}
        return copy(stat.at[k], stat_in.at[k], s_send.at[k], s_recv.at[k], device)

    rounds = peers.bit_length() - 1
    for k in range(rounds):
        stat_copy(k).start()
        stat_copy(k).wait_recv()
        top = jnp.maximum(stat[k, 0], stat_in[k, 0])
        stat[k + 1, 0] = top
        stat[k + 1, 1] = stat[k, 1] * jnp.exp(stat[k, 0] - top) + stat_in[k, 1] * jnp.exp(
            stat_in[k, 0] - top
        )
    stat[rounds, 1] = jnp.exp(stat[0, 0] - stat[rounds, 0]) / stat[rounds, 1]

    def widen(g, carry):
        rows = pl.ds(pl.multiple_of(g * block, block), block)
        row = jnp.broadcast_to(stat[rounds, 1, pl.ds(g, 1), :], (block, LANES))
        factor = jnp.sum(jnp.where(diagonal, row, 0.0), axis=1, keepdims=True)
        factor = jnp.broadcast_to(factor, (block, LANES))
        valid = valid_ref[pl.ds(pl.multiple_of(g * block, block) + rim, block), :] > 0
        f_ref[rows, :] = jnp.where(valid, factor, -1.0)
        return carry

    lax.fori_loop(0, ext // block, widen, 0)

    def map_gradient(c):
        first = (lane + c * chunk).astype(jnp.float32)

        def body(g, carry):
            for i in range(GROUPS):
                rows = pl.ds(pl.multiple_of(g * block + 8 * i, 8), 8)
                hit = jnp.where(lab_ref[rows, :] == first, 1.0, 0.0)
                factor = f_ref[rows, :]
                value = e_ref[c, rows, :] * jnp.maximum(factor, 0.0) - hit
                grad[c, rows, :] = jnp.where(factor >= 0.0, value, 0.0)
            return carry

        lax.fori_loop(0, ext // block, body, 0)

    def score_gradient(c):
        lengths = spread_filters(filt_ref, spread_taps(kern_ref, at(c))[::-1])
        spread_streams(lambda o: grad[c, pl.ds(o, 8, stride=4), :], strm_ref, ext // 32)

        def body(g, carry):
            base = pl.multiple_of(g * 8 * SPAN, 8)
            for p, sums in enumerate(fir(strm_ref, filt_ref, lengths, base, SPAN)):
                for k in range(SPAN):
                    turn[pl.ds(32 * k + p, 8, stride=4), :] = sums[k]
            rows = pl.ds(pl.multiple_of(g * 32 * SPAN, 32 * SPAN), 32 * SPAN)
            valid = f_ref[pl.ds(pl.multiple_of(g * 32 * SPAN, 32) + rim, 32 * SPAN), :] >= 0.0
            sg_ref[rows, at(c)] = jnp.where(valid, turn[...], 0.0).astype(jnp.bfloat16)
            return carry

        lax.fori_loop(0, row_count // (32 * SPAN), body, 0)

    def tap_gradient(c):
        def body(g, sums):
            base = pl.multiple_of(g * block, block)
            held = [grad[c, pl.ds(base + rim + 8 * i, 8), :] for i in range(GROUPS)]
            sums = list(sums)
            for o in range(8 * (GROUPS - 1) + taps_n):
                v = sc_ref[c, pl.ds(base + rim + o, 8), :]
                for i in range(GROUPS):
                    j = o - 8 * i
                    if 0 <= j < taps_n:
                        sums[j] = sums[j] + held[i] * v
            return tuple(sums)

        zero = jnp.zeros((8, LANES), jnp.float32)
        sums = lax.fori_loop(0, row_count // block, body, (zero,) * taps_n)
        for j in range(taps_n):
            kacc[c, j : j + 1, :] = jnp.sum(sums[j], axis=0, keepdims=True)

    def rec_copy(k, j):
        n = recs >> k
        theirs = (1 - my_bits[k]) * (n // 2)
        return copy(
            acc[k].at[pl.ds(theirs, n // 2), sub_at(j)],
            arrived[k].at[:, sub_at(j)],
            rec_send.at[k, j],
            rec_recv.at[k, j],
            {"rec": rec_peers[k]},
        )

    def summed(k, j):
        rec_copy(k, j).wait_recv()
        n = recs >> k
        mine = my_bits[k] * (n // 2)
        return acc[k][pl.ds(mine, n // 2), sub_at(j), :] + arrived[k][:, sub_at(j), :]

    def inward_copy(j, to_mid):
        big = inner if to_mid else outer
        recv = inn_recv if to_mid else out_recv
        return copy(mid.at[sub_at(j)], big.at[sub_at(j)], in_send.at[j], recv.at[j], {"tm": inward})

    def outward_copy(j):
        return copy(
            inner.at[sub_at(j)],
            inner.at[sub_at(j)],
            out_send.at[j],
            inn_recv.at[j],
            {"tm": outward},
        )

    def produce(c):
        map_gradient(c)
        score_gradient(c)
        part = lax.dot_general(
            sg_ref[:, at(c)],
            fr_ref[...],
            (((0,), (0,)), ((), ())),
            preferred_element_type=jnp.float32,
        )
        for p in range(recs):
            j = bit_reversed(p, bits)
            acc[0][p, at(c), :] = part[:, j * cols : (j + 1) * cols]
        for h in range(per):
            rec_copy(0, c * per + h).start()

    def exchange(k, j):
        acc[k][:, sub_at(j), :] = summed(k - 1, j)
        rec_copy(k, j).start()

    def gather_in(j):
        mid[sub_at(j), :] = summed(bits - 1, j)[0]

        @pl.when(jnp.logical_not(is_end))
        def _():
            inward_copy(j, False).wait_recv()
            mid[sub_at(j), :] += outer[sub_at(j), :]

        @pl.when(is_mid)
        def _():
            inward_copy(j, True).start()

        @pl.when(jnp.logical_not(is_mid))
        def _():
            inward_copy(j, False).start()

    def spread_out(j):
        inward_copy(j, True).wait_recv()

        @pl.when(is_mid)
        def _():
            inner[sub_at(j), :] += mid[sub_at(j), :]

        @pl.when(jnp.logical_not(is_end))
        def _():
            outward_copy(j).start()

        gq_ref[sub_at(j), :] = (inner[sub_at(j), :] * scale).astype(gq_ref.dtype)
        for k in range(bits):
            rec_copy(k, j).wait_send()
        inward_copy(j, False).wait_send()

    def k_copy(k, i):
        src = kacc.at[2 * i + 1 - my_bits[0]] if k == 0 else ksum.at[k - 1, i]
        return copy(src, karrived.at[k, i], k_send.at[k, i], k_recv.at[k, i], {"rec": rec_peers[k]})

    def k_summed(k, i):
        k_copy(k, i).wait_recv()
        own = kacc[2 * i + my_bits[0]] if k == 0 else ksum[k - 1, i]
        return own + karrived[k, i]

    def k_inward(i, to_mid):
        dst = kinner if to_mid else kouter
        recv = kinn_recv if to_mid else kout_recv
        return copy(kmid.at[i], dst.at[i], kin_send.at[i], recv.at[i], {"tm": inward})

    def k_outward(i):
        return copy(kinner.at[i], kinner.at[i], kout_send.at[i], kinn_recv.at[i], {"tm": outward})

    def k_give(i):
        return copy(kinner.at[i], kgot.at[i], kg_send.at[i], kg_recv.at[i], {"rec": rec_peers[0]})

    def k_exchange(k, i):
        ksum[k - 1, i] = k_summed(k - 1, i)
        k_copy(k, i).start()

    def k_gather(i):
        kmid[i] = k_summed(bits - 1, i)

        @pl.when(jnp.logical_not(is_end))
        def _():
            k_inward(i, False).wait_recv()
            kmid[i] += kouter[i]

        @pl.when(is_mid)
        def _():
            k_inward(i, True).start()

        @pl.when(jnp.logical_not(is_mid))
        def _():
            k_inward(i, False).start()

    def k_spread(i):
        k_inward(i, True).wait_recv()

        @pl.when(is_mid)
        def _():
            kinner[i] += kmid[i]

        k_give(i).start()

        @pl.when(jnp.logical_not(is_end))
        def _():
            k_outward(i).start()

        gk_ref[:, at(2 * i + my_bits[0])] = kinner[i]
        for k in range(bits):
            k_copy(k, i).wait_send()
        k_inward(i, False).wait_send()

    def k_take(i):
        k_give(i).wait_recv()
        gk_ref[:, at(2 * i + 1 - my_bits[0])] = kgot[i]

    reach = half - 1
    away = jnp.where(low, reach - t, t - half)

    def plan(step, first, spread, gather, swap, take):
        base = first + (bits - 1) * step
        ends = base + 2 * step * reach + step
        late = [(ends + first, take)] if take else []
        late += [(base + step * (reach + away + 1), spread), (base + step * (reach - away), gather)]
        late += [
            (first + (k - 1) * step, functools.partial(swap, k)) for k in range(bits - 1, 0, -1)
        ]
        return late, ends + (first if take else 0)

    stages, last = plan(hop, rate, spread_out, gather_in, exchange, None)
    k_stages, k_last = plan(tap_hop, 1, k_spread, k_gather, k_exchange, k_take)
    begun = 2 * count
    steps = begun + max((last + rate - 1) // rate, k_last)

    def step(s, carry):
        @pl.when(s < count)
        def _():
            produce(s)

        @pl.when(s == count)
        def _():
            for d in range(1, peers):
                f_compute(lax.rem(y + d, peers))
                f_copy(d).start()

        @pl.when(s == begun)
        def _():
            f_compute(y)

        c = s - count

        @pl.when((c >= 0) & (c < count))
        def _():
            tap_gradient(c)

            @pl.when(lax.rem(c, 2) == 1)
            def _():
                k_copy(0, c // 2).start()

        for i in range(rate):
            for delay, stage in stages:
                tick = s * rate + i - delay

                @pl.when((tick >= 0) & (tick < subs))
                def _(stage=stage, tick=tick):
                    stage(tick)

        for delay, stage in k_stages:
            tick = c - delay

            @pl.when((tick >= 0) & (tick < count) & (lax.rem(tick + 2, 2) == 1))
            def _(stage=stage, tick=tick):
                stage(tick // 2)

        return carry

    lax.fori_loop(0, steps, step, 0)

    for d in range(1, peers):
        f_copy(d).wait_recv()
    total = fpart[y]
    for d in range(1, peers):
        total = total + fin[d - 1]
    gf_ref[...] = (total * scale).astype(gf_ref.dtype)
    for d in range(1, peers):
        f_copy(d).wait_send()

    @pl.when(jnp.logical_not(is_end))
    def _():
        def drain(j, carry):
            outward_copy(j).wait_send()
            return carry

        lax.fori_loop(0, subs, drain, 0)

    def k_drain(i, carry):
        k_give(i).wait_send()

        @pl.when(jnp.logical_not(is_end))
        def _():
            k_outward(i).wait_send()

        return carry

    lax.fori_loop(0, count // 2, k_drain, 0)
    for k in range(rounds):
        stat_copy(k).wait_send()
    for side in range(2):
        @pl.when(has[side])
        def _(side=side):
            for one in halo_copies(side):
                one.wait_send()


SPLIT = 2
HOP = 3
TAP_HOP = 3
PARTS = 2


def gradients(labels, lengths, frame_rows, queries, kernel, scale):
    tms, peers, recs = (lax.axis_size("tm"), lax.axis_size("query"), lax.axis_size("rec"))
    bits = recs.bit_length() - 1
    row_count, width = frame_rows.shape
    query_count = queries.shape[0]
    taps = kernel.shape[0]
    chunk = LANES
    sub = chunk // SPLIT
    count = query_count // chunk
    subs = query_count // sub
    cols, fcols = (width // recs, width // peers)
    rim = taps // 2
    ext, wide = (row_count + 2 * rim, row_count + 4 * rim)
    rounds = peers.bit_length() - 1
    stat_rows = (ext // (8 * GROUPS) + 7) // 8 * 8
    pairs = count // 2
    f32 = jnp.float32
    vmem = pltpu.VMEM
    small = vmem((pairs, taps, chunk), f32)
    block = vmem((query_count, cols), f32)
    scratch = [vmem((recs >> k, query_count, cols), f32) for k in range(bits)]
    scratch += [vmem((recs >> (k + 1), query_count, cols), f32) for k in range(bits)]
    scratch += [
        vmem((count, taps, chunk), f32),
        vmem((max(bits - 1, 1), pairs, taps, chunk), f32),
        vmem((bits, pairs, taps, chunk), f32),
    ]
    scratch += [block] * 3 + [small] * 4
    scratch += [
        vmem((peers, row_count, fcols), f32),
        vmem((peers - 1, row_count, fcols), f32),
        vmem((row_count, query_count), jnp.bfloat16),
        vmem((count, ext + 8, chunk), f32),
        vmem((count, wide + 8, chunk), f32),
        vmem((count, ext, chunk), f32),
        vmem((ext, chunk), f32),
        vmem((ext, chunk), f32),
        vmem((wide, chunk), f32),
        vmem((4 * rim, width), jnp.bfloat16),
        vmem((2, 2 * rim, width), f32),
        vmem((2, 2 * rim, width), f32),
        vmem((rounds + 1, 2, stat_rows, LANES), f32),
        vmem((rounds, 2, stat_rows, LANES), f32),
        vmem((row_count, width), jnp.bfloat16),
        vmem((query_count, width), jnp.bfloat16),
        vmem((taps, query_count), f32),
        vmem((1, row_count), jnp.int32),
        vmem((2, 1, row_count), jnp.int32),
        pltpu.SMEM((1,), jnp.int32),
        vmem((9, wide // 4, chunk), f32),
        vmem((9 * (taps // 4 + 1), 8, chunk), f32),
        vmem((32 * SPAN, chunk), f32),
    ]
    dma = pltpu.SemaphoreType.DMA
    scratch += [dma((bits, subs))] * 2 + [dma((subs,))] * 4 + [dma((peers - 1,))] * 2
    scratch += [dma((2, 2))] * 2 + [dma((rounds,))] * 2 + [dma((4,)), dma((PARTS,))]
    scratch += [dma((bits, pairs))] * 2 + [dma((pairs,))] * 6
    hbm = pl.BlockSpec(memory_space=pl.ANY)
    dims = (tms, peers, recs, chunk, sub, HOP, TAP_HOP)
    return pl.pallas_call(
        functools.partial(gradient_kernel, dims, scale),
        out_shape=(
            pltpu.VMEM((row_count, fcols), jnp.bfloat16),
            pltpu.VMEM((query_count, cols), jnp.bfloat16),
            pltpu.VMEM((taps, query_count), f32),
        ),
        in_specs=[hbm] * 5,
        out_specs=(pl.BlockSpec(memory_space=pltpu.VMEM),) * 3,
        scratch_shapes=scratch,
        compiler_params=pltpu.CompilerParams(
            collective_id=0, has_side_effects=True, vmem_limit_bytes=60 * 1024 * 1024
        ),
        name="gradients",
    )(labels, lengths, frame_rows, queries, kernel)


def store_kernel(*refs):
    ins, outs, sem = refs[:3], refs[3:6], refs[6]
    copies = [pltpu.make_async_copy(a, b, sem.at[i]) for i, (a, b) in enumerate(zip(ins, outs))]
    for one in copies:
        one.start()
    for one in copies:
        one.wait()


def store(arrays):
    return pl.pallas_call(
        store_kernel,
        out_shape=tuple(jax.ShapeDtypeStruct(a.shape, a.dtype) for a in arrays),
        in_specs=[pl.BlockSpec(memory_space=pltpu.VMEM)] * 3,
        out_specs=(pl.BlockSpec(memory_space=pl.ANY),) * 3,
        scratch_shapes=[pltpu.SemaphoreType.DMA((3,))],
        compiler_params=pltpu.CompilerParams(vmem_limit_bytes=4 * 1024 * 1024),
        name="store",
    )(*arrays)


def per_device(frames, queries, kernel, labels, lengths):
    frame_rows = frames[0]
    width = frame_rows.shape[1]
    logit_scale = 10.0 / math.sqrt(width)
    grad_frames, grad_queries, grad_kernel = store(
        gradients(labels, lengths, frame_rows, queries, kernel, logit_scale)
    )
    return (grad_frames[None], grad_queries, grad_kernel)


def solution(mesh):
    in_specs = (P("rec", "tm", None), P("query", None), P(None, "query"), P("rec", "tm"), P("rec"))
    out_specs = (P("rec", "tm", "query"), P("query", "rec"), P(None, "query"))
    return jax.shard_map(
        per_device, mesh=mesh, in_specs=in_specs, out_specs=out_specs, check_vma=False
    )
```

```python
import functools
import math

import jax
import jax.numpy as jnp
from jax import lax
from jax.experimental import pallas as pl
from jax.experimental.pallas import tpu as pltpu
from jax.sharding import PartitionSpec as P


GROUPS = 4
LANES = 128


def spread_taps(kern_ref, lanes):
    taps = kern_ref.shape[0]
    return [jnp.broadcast_to(kern_ref[j : j + 1, lanes], (8, LANES)) for j in range(taps)]


SPAN = 4
AHEAD = 3


def plus(a, b):
    return [x + b[i] if i < len(b) else x for i, x in enumerate(a)]


def minus(a):
    return [-x for x in a]


def spread_filters(filt_ref, h):
    even, odd = h[0::2], h[1::2]
    both = plus(even, odd)
    filters = (
        plus(both[0::2], both[1::2]),
        both[0::2],
        minus(both[1::2]),
        plus(even[0::2], even[1::2]),
        even[0::2],
        minus(even[1::2]),
        minus(plus(odd[0::2], odd[1::2])),
        minus(odd[0::2]),
        odd[1::2],
    )
    depth = len(filters[0])
    for n, one in enumerate(filters):
        for i, x in enumerate(one):
            filt_ref[n * depth + i] = x
    return [len(one) for one in filters]


def spread_streams(load, strm_ref, groups):
    def one_group(g):
        x = [load(pl.multiple_of(g * 32, 32) + o) for o in range(7)]
        e = [x[o] - x[o + 2] for o in range(5)]
        f = [e[o] - e[o + 1] for o in range(4)]
        rows = pl.ds(pl.multiple_of(g * 8, 8), 8)
        streams = (x[3], e[1], e[3], x[2] - x[3], f[0], f[2], x[3] - x[4], f[1], f[3])
        for n, one in enumerate(streams):
            strm_ref[n, rows, :] = one

    def body(i, carry):
        for k in range(AHEAD):
            one_group(i * AHEAD + k)
        return carry

    lax.fori_loop(0, groups // AHEAD, body, 0)
    for g in range(groups // AHEAD * AHEAD, groups):
        one_group(g)


def fir(strm_ref, filt_ref, lengths, base, span):
    depth = lengths[0]
    done = []
    for n, count in enumerate(lengths):
        taps = [filt_ref[n * depth + i] for i in range(count)]
        sums = list(done[n // 3 * 3]) if n % 3 else [None] * span
        for o in range(8 * (span - 1) + count):
            v = strm_ref[n, pl.ds(base + o, 8), :]
            for k in range(span):
                i = o - 8 * k
                if 0 <= i < count:
                    term = taps[i] * v
                    sums[k] = term if sums[k] is None else sums[k] + term
        done.append(sums)
    add = lambda a, b: [x + z for x, z in zip(a, b)]
    return (
        add(done[1], done[4]),
        add(done[1], done[7]),
        add(done[2], done[5]),
        add(done[2], done[8]),
    )


MESH = pl.DeviceIdType.MESH


def bit_reversed(p, bits):
    return sum(((p >> k) & 1) << (bits - 1 - k) for k in range(bits))


def gradient_kernel(dims, scale, lab_hbm, len_hbm, fr_hbm, qu_hbm, kern_hbm, *refs):
    tms, peers, recs, chunk, sub, hop, tap_hop = dims
    bits = recs.bit_length() - 1
    gf_ref, gq_ref, gk_ref = refs[:3]
    scratch = refs[3:]
    acc, scratch = scratch[:bits], scratch[bits:]
    arrived, scratch = scratch[:bits], scratch[bits:]
    kacc, ksum, karrived, scratch = (scratch[0], scratch[1], scratch[2], scratch[3:])
    (mid, outer, inner, kmid, kouter, kinner, kgot, fpart, fin, sg_ref, grad) = scratch[:11]
    (sc_ref, e_ref, f_ref, lab_ref, valid_ref, xh_ref, hin, hout, stat, stat_in) = scratch[11:21]
    (fr_ref, qu_ref, kern_ref, lab_row, lab_in, len_ref, strm_ref, filt_ref, turn) = scratch[21:30]
    edge_ref, scratch = scratch[30], scratch[31:]
    (rec_send, rec_recv, in_send, out_recv, out_send, inn_recv, f_send, f_recv) = scratch[:8]
    (h_send, h_recv, s_send, s_recv, load_sem, qu_sem) = scratch[8:14]
    (k_send, k_recv, kin_send, kout_recv, kout_send, kinn_recv, kg_send, kg_recv) = scratch[14:]

    t = lax.axis_index("tm")
    y = lax.axis_index("query")
    r = lax.axis_index("rec")
    half = tms // 2
    low = t < half
    is_end = (t == 0) | (t == tms - 1)
    is_mid = (t == half - 1) | (t == half)
    inward = jnp.where(low, t + 1, t - 1)
    outward = jnp.where(low, lax.rem(t + tms - 1, tms), lax.rem(t + 1, tms))
    my_bits = [lax.rem(r // (1 << k), 2) for k in range(bits)]
    rec_peers = [r + (1 - 2 * my_bits[k]) * (1 << k) for k in range(bits)]

    barrier = pltpu.get_barrier_semaphore()

    def greet(device):
        pl.semaphore_signal(barrier, inc=1, device_id=device, device_id_type=MESH)

    for peer in rec_peers:
        greet({"rec": peer})
    for d in range(1, peers):
        greet({"query": lax.rem(y + d, peers)})
    greet({"tm": inward})

    @pl.when(jnp.logical_not(is_end))
    def _():
        greet({"tm": outward})

    edges = [slice(0, 2 * (kern_ref.shape[0] // 2))]
    edges.append(slice(fr_ref.shape[0] - edges[0].stop, fr_ref.shape[0]))
    edge_loads = [
        pltpu.make_async_copy(fr_hbm.at[rows], edge_ref.at[side], load_sem.at[4 + side])
        for side, rows in enumerate(edges)
    ]
    loads = [
        pltpu.make_async_copy(src, dst, load_sem.at[i])
        for i, (src, dst) in enumerate(
            ((fr_hbm, fr_ref), (lab_hbm, lab_row), (len_hbm, len_ref), (kern_hbm, kern_ref))
        )
    ]
    queries, width = qu_ref.shape
    parts = qu_sem.shape[0]
    span = queries // parts

    def qu_load(p):
        rows = pl.ds(p * span, span)
        return pltpu.make_async_copy(qu_hbm.at[rows], qu_ref.at[rows], qu_sem.at[p])

    for one in edge_loads + loads[1:3] + loads[:1]:
        one.start()
    for p in range(parts):
        qu_load(p).start()
    loads[3].start()

    count = queries // chunk
    subs = queries // sub
    per = chunk // sub
    rate = per // 2
    cols = width // recs
    fcols = width // peers
    row_count = sg_ref.shape[0]
    f_tiles = row_count // LANES
    taps_n = kern_ref.shape[0]
    rim = taps_n // 2
    halo = 2 * rim
    block = 8 * GROUPS
    ext = f_ref.shape[0]
    tiles = e_ref.shape[0]
    wide = valid_ref.shape[0]
    lane = lax.broadcasted_iota(jnp.int32, (8, LANES), 1) + y * queries

    def copy(src, dst, send, recv, device):
        return pltpu.make_async_remote_copy(
            src_ref=src,
            dst_ref=dst,
            send_sem=send,
            recv_sem=recv,
            device_id=device,
            device_id_type=MESH,
        )

    def at(c):
        return pl.ds(pl.multiple_of(c * chunk, chunk), chunk)

    def sub_at(j):
        return pl.ds(pl.multiple_of(j * sub, sub), sub)

    def f_rows(i):
        return pl.ds(pl.multiple_of(i * LANES, LANES), LANES)

    def f_copy(d, i):
        p = lax.rem(y + d, peers)
        return copy(
            fpart.at[p, f_rows(i)],
            fin.at[d - 1, f_rows(i)],
            f_send.at[d - 1, i],
            f_recv.at[d - 1, i],
            {"query": p},
        )

    def f_compute(p, i):
        columns = pl.ds(pl.multiple_of(p * fcols, fcols), fcols)
        fpart[p, f_rows(i), :] = jnp.dot(
            sg_ref[f_rows(i), :], qu_ref[:, columns], preferred_element_type=jnp.float32
        )

    def f_finish():
        for i in range(f_tiles):
            for d in range(1, peers):
                f_copy(d, i).wait_recv()
        total = fpart[y]
        for d in range(1, peers):
            total = total + fin[d - 1]
        gf_ref[...] = (total * scale).astype(gf_ref.dtype)
        for i in range(f_tiles):
            for d in range(1, peers):
                f_copy(d, i).wait_send()

    has = [t > 0, t < tms - 1]

    def halo_copies(side):
        device = {"tm": lax.rem(t + (tms - 1 if side == 0 else 1), tms)}
        return (
            copy(
                hout.at[side],
                hin.at[1 - side],
                h_send.at[0, side],
                h_recv.at[0, 1 - side],
                device,
            ),
            copy(
                lab_row,
                lab_in.at[1 - side],
                h_send.at[1, side],
                h_recv.at[1, 1 - side],
                device,
            ),
        )

    for side in range(2):
        edge_loads[side].wait()
        hout[side] = edge_ref[side].astype(jnp.float32)
    loads[1].wait()
    pl.semaphore_wait(barrier, jnp.where(is_end, bits + peers, bits + peers + 1))

    for side in range(2):
        @pl.when(has[side])
        def _(side=side):
            for one in halo_copies(side):
                one.start()

    loads[2].wait()
    frame = lax.broadcasted_iota(jnp.int32, (wide, LANES), 0) + (t * row_count - halo)
    valid_ref[...] = jnp.where((frame >= 0) & (frame < len_ref[0]), 1.0, 0.0)
    stat[...] = jnp.zeros_like(stat)

    def column_of(row):
        return jnp.transpose(jnp.broadcast_to(row.astype(jnp.float32), (LANES, LANES)))

    for i in range(row_count // LANES):
        lab_ref[rim + i * LANES : rim + (i + 1) * LANES, :] = column_of(
            lab_row[:, i * LANES : (i + 1) * LANES]
        )

    batch = min(BATCH, tiles // parts)

    def score(rows_of, keep):
        def body(c, carry):
            rows = pl.ds(pl.multiple_of(c * batch * LANES, LANES), batch * LANES)
            part = lax.dot_general(
                rows_of[...],
                qu_ref[rows, :],
                (((1,), (1,)), ((), ())),
                preferred_element_type=jnp.float32,
            )
            for h in range(batch):
                for begin, rows in keep:
                    size = rows.stop - rows.start
                    one = part[begin : begin + size, h * LANES : (h + 1) * LANES] * scale
                    one = jnp.where(valid_ref[rows, :] > 0, one, 0.0)
                    sc_ref[batch * c + h, rows, :] = one
            return carry

        return body

    loads[0].wait()
    each = tiles // batch // parts
    own_rows = slice(halo, halo + row_count)
    for p in range(parts):
        qu_load(p).wait()
        lax.fori_loop(p * each, (p + 1) * each, score(fr_ref, [(0, own_rows)]), 0)

    for side in range(2):
        @pl.when(has[side])
        def _(side=side):
            for one in halo_copies(1 - side):
                one.wait_recv()

        @pl.when(jnp.logical_not(has[side]))
        def _(side=side):
            hin[side] = jnp.zeros((halo, width), jnp.float32)
            lab_in[side] = jnp.zeros((1, row_count), jnp.int32)

    xh_ref[:halo, :] = hin[0].astype(jnp.bfloat16)
    xh_ref[halo:, :] = hin[1].astype(jnp.bfloat16)
    lab_ref[:rim, :] = column_of(lab_in[0, :, row_count - LANES :])[LANES - rim :, :]
    lab_ref[rim + row_count :, :] = column_of(lab_in[1, :, :LANES])[:rim, :]

    outer_rows = [(0, slice(0, halo)), (halo, slice(halo + row_count, wide))]
    lax.fori_loop(0, tiles // batch, score(xh_ref, outer_rows), 0)
    loads[3].wait()

    def smoothed(c, carry):
        lengths = spread_filters(filt_ref, spread_taps(kern_ref, at(c)))
        spread_streams(lambda o: sc_ref[c, pl.ds(o, 8, stride=4), :], strm_ref, wide // 32)

        def piece(base, span):
            for p, sums in enumerate(fir(strm_ref, filt_ref, lengths, base, span)):
                for k in range(span):
                    rows = pl.ds(4 * base + 32 * k + p, 8, stride=4)
                    e_ref[c, rows, :] = sums[k]

        def body(g, carry):
            piece(pl.multiple_of(g * 8 * SPAN, 8), SPAN)
            return carry

        whole = ext // (32 * SPAN)
        lax.fori_loop(0, whole, body, 0)
        for g in range(whole * SPAN, ext // 32):
            piece(8 * g, 1)
        return carry

    lax.fori_loop(0, tiles, smoothed, 0)

    diagonal = lax.broadcasted_iota(jnp.int32, (block, LANES), 0) == lax.broadcasted_iota(
        jnp.int32, (block, LANES), 1
    )

    def widest(g, carry):
        rows = pl.ds(pl.multiple_of(g * block, block), block)
        top = e_ref[0, rows, :]
        for c in range(1, tiles):
            top = jnp.maximum(top, e_ref[c, rows, :])
        f_ref[rows, :] = top
        return carry

    lax.fori_loop(0, ext // block, widest, 0)

    def note(i, g, value):
        picked = jnp.where(diagonal, value, 0.0)
        stat[0, i, pl.ds(g, 1), :] = jnp.sum(picked, axis=0, keepdims=True)

    for g in range(ext // block):
        rows = pl.ds(g * block, block)
        top = jnp.max(f_ref[rows, :], axis=1, keepdims=True)
        top = jnp.broadcast_to(top, (block, LANES))
        f_ref[rows, :] = top
        note(0, g, top)

    def exponents(g, carry):
        rows = pl.ds(pl.multiple_of(g * block, block), block)
        top = f_ref[rows, :]
        total = jnp.zeros((block, LANES), jnp.float32)
        for c in range(tiles):
            e = jnp.exp(e_ref[c, rows, :] - top)
            e_ref[c, rows, :] = e
            total = total + e
        f_ref[rows, :] = total
        return carry

    lax.fori_loop(0, ext // block, exponents, 0)

    for g in range(ext // block):
        total = jnp.sum(f_ref[pl.ds(g * block, block), :], axis=1, keepdims=True)
        note(1, g, jnp.broadcast_to(total, (block, LANES)))

    def stat_copy(k):
        bit = lax.rem(y // (1 << k), 2)
        device = {"query": y + (1 - 2 * bit) * (1 << k)}
        return copy(stat.at[k], stat_in.at[k], s_send.at[k], s_recv.at[k], device)

    rounds = peers.bit_length() - 1
    for k in range(rounds):
        stat_copy(k).start()
        stat_copy(k).wait_recv()
        top = jnp.maximum(stat[k, 0], stat_in[k, 0])
        stat[k + 1, 0] = top
        stat[k + 1, 1] = stat[k, 1] * jnp.exp(stat[k, 0] - top) + stat_in[k, 1] * jnp.exp(
            stat_in[k, 0] - top
        )
    stat[rounds, 1] = jnp.exp(stat[0, 0] - stat[rounds, 0]) / stat[rounds, 1]

    for g in range(ext // block):
        rows = pl.ds(g * block, block)
        row = jnp.broadcast_to(stat[rounds, 1, g : g + 1, :], (block, LANES))
        factor = jnp.sum(jnp.where(diagonal, row, 0.0), axis=1, keepdims=True)
        factor = jnp.broadcast_to(factor, (block, LANES))
        valid = valid_ref[pl.ds(g * block + rim, block), :] > 0
        f_ref[rows, :] = jnp.where(valid, factor, -1.0)

    def map_gradient(c):
        first = (lane + c * chunk).astype(jnp.float32)

        def body(g, carry):
            for i in range(GROUPS):
                rows = pl.ds(pl.multiple_of(g * block + 8 * i, 8), 8)
                hit = jnp.where(lab_ref[rows, :] == first, 1.0, 0.0)
                factor = f_ref[rows, :]
                value = e_ref[c, rows, :] * jnp.maximum(factor, 0.0) - hit
                grad[c, rows, :] = jnp.where(factor >= 0.0, value, 0.0)
            return carry

        lax.fori_loop(0, ext // block, body, 0)

    def score_gradient(c):
        lengths = spread_filters(filt_ref, spread_taps(kern_ref, at(c))[::-1])
        spread_streams(lambda o: grad[c, pl.ds(o, 8, stride=4), :], strm_ref, ext // 32)

        def body(g, carry):
            base = pl.multiple_of(g * 8 * SPAN, 8)
            for p, sums in enumerate(fir(strm_ref, filt_ref, lengths, base, SPAN)):
                for k in range(SPAN):
                    turn[pl.ds(32 * k + p, 8, stride=4), :] = sums[k]
            rows = pl.ds(pl.multiple_of(g * 32 * SPAN, 32 * SPAN), 32 * SPAN)
            valid = f_ref[pl.ds(pl.multiple_of(g * 32 * SPAN, 32) + rim, 32 * SPAN), :] >= 0.0
            sg_ref[rows, at(c)] = jnp.where(valid, turn[...], 0.0).astype(jnp.bfloat16)
            return carry

        lax.fori_loop(0, row_count // (32 * SPAN), body, 0)

    def tap_gradient(c):
        def body(g, sums):
            base = pl.multiple_of(g * block, block)
            held = [grad[c, pl.ds(base + rim + 8 * i, 8), :] for i in range(GROUPS)]
            sums = list(sums)
            for o in range(8 * (GROUPS - 1) + taps_n):
                v = sc_ref[c, pl.ds(base + rim + o, 8), :]
                for i in range(GROUPS):
                    j = o - 8 * i
                    if 0 <= j < taps_n:
                        sums[j] = sums[j] + held[i] * v
            return tuple(sums)

        zero = jnp.zeros((8, LANES), jnp.float32)
        sums = lax.fori_loop(0, row_count // block, body, (zero,) * taps_n)
        for j in range(taps_n):
            kacc[c, j : j + 1, :] = jnp.sum(sums[j], axis=0, keepdims=True)

    def rec_copy(k, j):
        n = recs >> k
        theirs = (1 - my_bits[k]) * (n // 2)
        return copy(
            acc[k].at[pl.ds(theirs, n // 2), sub_at(j)],
            arrived[k].at[:, sub_at(j)],
            rec_send.at[k, j],
            rec_recv.at[k, j],
            {"rec": rec_peers[k]},
        )

    def summed(k, j):
        rec_copy(k, j).wait_recv()
        n = recs >> k
        mine = my_bits[k] * (n // 2)
        return acc[k][pl.ds(mine, n // 2), sub_at(j), :] + arrived[k][:, sub_at(j), :]

    def inward_copy(j, to_mid):
        big = inner if to_mid else outer
        recv = inn_recv if to_mid else out_recv
        return copy(mid.at[sub_at(j)], big.at[sub_at(j)], in_send.at[j], recv.at[j], {"tm": inward})

    def outward_copy(j):
        return copy(
            inner.at[sub_at(j)],
            inner.at[sub_at(j)],
            out_send.at[j],
            inn_recv.at[j],
            {"tm": outward},
        )

    def produce(c):
        map_gradient(c)
        score_gradient(c)
        part = lax.dot_general(
            sg_ref[:, at(c)],
            fr_ref[...],
            (((0,), (0,)), ((), ())),
            preferred_element_type=jnp.float32,
        )
        for p in range(recs):
            j = bit_reversed(p, bits)
            acc[0][p, at(c), :] = part[:, j * cols : (j + 1) * cols]
        for h in range(per):
            rec_copy(0, c * per + h).start()

    def exchange(k, j):
        acc[k][:, sub_at(j), :] = summed(k - 1, j)
        rec_copy(k, j).start()

    def gather_in(j):
        mid[sub_at(j), :] = summed(bits - 1, j)[0]

        @pl.when(jnp.logical_not(is_end))
        def _():
            inward_copy(j, False).wait_recv()
            mid[sub_at(j), :] += outer[sub_at(j), :]

        @pl.when(is_mid)
        def _():
            inward_copy(j, True).start()

        @pl.when(jnp.logical_not(is_mid))
        def _():
            inward_copy(j, False).start()

    def spread_out(j):
        inward_copy(j, True).wait_recv()

        @pl.when(is_mid)
        def _():
            inner[sub_at(j), :] += mid[sub_at(j), :]

        @pl.when(jnp.logical_not(is_end))
        def _():
            outward_copy(j).start()

        gq_ref[sub_at(j), :] = (inner[sub_at(j), :] * scale).astype(gq_ref.dtype)
        for k in range(bits):
            rec_copy(k, j).wait_send()
        inward_copy(j, False).wait_send()

    def k_copy(k, i):
        src = kacc.at[2 * i + 1 - my_bits[0]] if k == 0 else ksum.at[k - 1, i]
        return copy(src, karrived.at[k, i], k_send.at[k, i], k_recv.at[k, i], {"rec": rec_peers[k]})

    def k_summed(k, i):
        k_copy(k, i).wait_recv()
        own = kacc[2 * i + my_bits[0]] if k == 0 else ksum[k - 1, i]
        return own + karrived[k, i]

    def k_inward(i, to_mid):
        dst = kinner if to_mid else kouter
        recv = kinn_recv if to_mid else kout_recv
        return copy(kmid.at[i], dst.at[i], kin_send.at[i], recv.at[i], {"tm": inward})

    def k_outward(i):
        return copy(kinner.at[i], kinner.at[i], kout_send.at[i], kinn_recv.at[i], {"tm": outward})

    def k_give(i):
        return copy(kinner.at[i], kgot.at[i], kg_send.at[i], kg_recv.at[i], {"rec": rec_peers[0]})

    def k_exchange(k, i):
        ksum[k - 1, i] = k_summed(k - 1, i)
        k_copy(k, i).start()

    def k_gather(i):
        kmid[i] = k_summed(bits - 1, i)

        @pl.when(jnp.logical_not(is_end))
        def _():
            k_inward(i, False).wait_recv()
            kmid[i] += kouter[i]

        @pl.when(is_mid)
        def _():
            k_inward(i, True).start()

        @pl.when(jnp.logical_not(is_mid))
        def _():
            k_inward(i, False).start()

    def k_spread(i):
        k_inward(i, True).wait_recv()

        @pl.when(is_mid)
        def _():
            kinner[i] += kmid[i]

        k_give(i).start()

        @pl.when(jnp.logical_not(is_end))
        def _():
            k_outward(i).start()

        gk_ref[:, at(2 * i + my_bits[0])] = kinner[i]
        for k in range(bits):
            k_copy(k, i).wait_send()
        k_inward(i, False).wait_send()

    def k_take(i):
        k_give(i).wait_recv()
        gk_ref[:, at(2 * i + 1 - my_bits[0])] = kgot[i]

    reach = half - 1
    away = jnp.where(low, reach - t, t - half)

    def plan(step, first, spread, gather, swap, take):
        base = first + (bits - 1) * step
        ends = base + 2 * step * reach + step
        late = [(ends + first, take)] if take else []
        late += [(base + step * (reach + away + 1), spread), (base + step * (reach - away), gather)]
        late += [
            (first + (k - 1) * step, functools.partial(swap, k)) for k in range(bits - 1, 0, -1)
        ]
        return late, ends + (first if take else 0)

    stages, last = plan(hop, rate, spread_out, gather_in, exchange, None)
    k_stages, k_last = plan(tap_hop, 1, k_spread, k_gather, k_exchange, k_take)
    begun = 2 * count
    f_end = max(begun + 4, count + peers * f_tiles)
    steps = max(begun + (last + rate - 1) // rate, begun + k_last, f_end + 1)

    def step(s, carry):
        @pl.when(s < count)
        def _():
            produce(s)

        c = s - count

        @pl.when((c >= 0) & (c < peers * f_tiles))
        def _():
            p = lax.rem(y + 1 + c // f_tiles, peers)
            f_compute(p, lax.rem(c, f_tiles))

            for d in range(1, peers):
                @pl.when(c // f_tiles == d - 1)
                def _(d=d):
                    f_copy(d, lax.rem(c, f_tiles)).start()

        @pl.when(s == f_end)
        def _():
            f_finish()

        @pl.when((c >= 0) & (c < count))
        def _():
            tap_gradient(c)

            @pl.when(lax.rem(c, 2) == 1)
            def _():
                k_copy(0, c // 2).start()

        for i in range(rate):
            for delay, stage in stages:
                tick = s * rate + i - delay

                @pl.when((tick >= 0) & (tick < subs))
                def _(stage=stage, tick=tick):
                    stage(tick)

        for delay, stage in k_stages:
            tick = c - delay

            @pl.when((tick >= 0) & (tick < count) & (lax.rem(tick + 2, 2) == 1))
            def _(stage=stage, tick=tick):
                stage(tick // 2)

        return carry

    lax.fori_loop(0, steps, step, 0)

    @pl.when(jnp.logical_not(is_end))
    def _():
        def drain(j, carry):
            outward_copy(j).wait_send()
            return carry

        lax.fori_loop(0, subs, drain, 0)

    def k_drain(i, carry):
        k_give(i).wait_send()

        @pl.when(jnp.logical_not(is_end))
        def _():
            k_outward(i).wait_send()

        return carry

    lax.fori_loop(0, count // 2, k_drain, 0)
    for k in range(rounds):
        stat_copy(k).wait_send()
    for side in range(2):
        @pl.when(has[side])
        def _(side=side):
            for one in halo_copies(side):
                one.wait_send()


SPLIT = 2
HOP = 3
TAP_HOP = 3
PARTS = 2
BATCH = 4


def gradients(labels, lengths, frame_rows, queries, kernel, scale):
    tms, peers, recs = (lax.axis_size("tm"), lax.axis_size("query"), lax.axis_size("rec"))
    bits = recs.bit_length() - 1
    row_count, width = frame_rows.shape
    query_count = queries.shape[0]
    taps = kernel.shape[0]
    chunk = LANES
    sub = chunk // SPLIT
    count = query_count // chunk
    subs = query_count // sub
    cols, fcols = (width // recs, width // peers)
    rim = taps // 2
    ext, wide = (row_count + 2 * rim, row_count + 4 * rim)
    rounds = peers.bit_length() - 1
    stat_rows = (ext // (8 * GROUPS) + 7) // 8 * 8
    pairs = count // 2
    f32 = jnp.float32
    vmem = pltpu.VMEM
    small = vmem((pairs, taps, chunk), f32)
    block = vmem((query_count, cols), f32)
    scratch = [vmem((recs >> k, query_count, cols), f32) for k in range(bits)]
    scratch += [vmem((recs >> (k + 1), query_count, cols), f32) for k in range(bits)]
    scratch += [
        vmem((count, taps, chunk), f32),
        vmem((max(bits - 1, 1), pairs, taps, chunk), f32),
        vmem((bits, pairs, taps, chunk), f32),
    ]
    scratch += [block] * 3 + [small] * 4
    scratch += [
        vmem((peers, row_count, fcols), f32),
        vmem((peers - 1, row_count, fcols), f32),
        vmem((row_count, query_count), jnp.bfloat16),
        vmem((count, ext + 8, chunk), f32),
        vmem((count, wide + 8, chunk), f32),
        vmem((count, ext, chunk), f32),
        vmem((ext, chunk), f32),
        vmem((ext, chunk), f32),
        vmem((wide, chunk), f32),
        vmem((4 * rim, width), jnp.bfloat16),
        vmem((2, 2 * rim, width), f32),
        vmem((2, 2 * rim, width), f32),
        vmem((rounds + 1, 2, stat_rows, LANES), f32),
        vmem((rounds, 2, stat_rows, LANES), f32),
        vmem((row_count, width), jnp.bfloat16),
        vmem((query_count, width), jnp.bfloat16),
        vmem((taps, query_count), f32),
        vmem((1, row_count), jnp.int32),
        vmem((2, 1, row_count), jnp.int32),
        pltpu.SMEM((1,), jnp.int32),
        vmem((9, wide // 4, chunk), f32),
        vmem((9 * (taps // 4 + 1), 8, chunk), f32),
        vmem((32 * SPAN, chunk), f32),
        vmem((2, 2 * rim, width), jnp.bfloat16),
    ]
    dma = pltpu.SemaphoreType.DMA
    scratch += [dma((bits, subs))] * 2 + [dma((subs,))] * 4 + [dma((peers - 1, row_count // LANES))] * 2
    scratch += [dma((2, 2))] * 2 + [dma((rounds,))] * 2 + [dma((6,)), dma((PARTS,))]
    scratch += [dma((bits, pairs))] * 2 + [dma((pairs,))] * 6
    hbm = pl.BlockSpec(memory_space=pl.ANY)
    dims = (tms, peers, recs, chunk, sub, HOP, TAP_HOP)
    return pl.pallas_call(
        functools.partial(gradient_kernel, dims, scale),
        out_shape=(
            pltpu.VMEM((row_count, fcols), jnp.bfloat16),
            pltpu.VMEM((query_count, cols), jnp.bfloat16),
            pltpu.VMEM((taps, query_count), f32),
        ),
        in_specs=[hbm] * 5,
        out_specs=(pl.BlockSpec(memory_space=pltpu.VMEM),) * 3,
        scratch_shapes=scratch,
        compiler_params=pltpu.CompilerParams(
            collective_id=0, has_side_effects=True, vmem_limit_bytes=60 * 1024 * 1024
        ),
        name="gradients",
    )(labels, lengths, frame_rows, queries, kernel)


def store_kernel(*refs):
    ins, outs, sem = refs[:3], refs[3:6], refs[6]
    copies = [pltpu.make_async_copy(a, b, sem.at[i]) for i, (a, b) in enumerate(zip(ins, outs))]
    for one in copies:
        one.start()
    for one in copies:
        one.wait()


def store(arrays):
    return pl.pallas_call(
        store_kernel,
        out_shape=tuple(jax.ShapeDtypeStruct(a.shape, a.dtype) for a in arrays),
        in_specs=[pl.BlockSpec(memory_space=pltpu.VMEM)] * 3,
        out_specs=(pl.BlockSpec(memory_space=pl.ANY),) * 3,
        scratch_shapes=[pltpu.SemaphoreType.DMA((3,))],
        compiler_params=pltpu.CompilerParams(vmem_limit_bytes=4 * 1024 * 1024),
        name="store",
    )(*arrays)


def per_device(frames, queries, kernel, labels, lengths):
    frame_rows = frames[0]
    width = frame_rows.shape[1]
    logit_scale = 10.0 / math.sqrt(width)
    grad_frames, grad_queries, grad_kernel = store(
        gradients(labels, lengths, frame_rows, queries, kernel, logit_scale)
    )
    return (grad_frames[None], grad_queries, grad_kernel)


def solution(mesh):
    in_specs = (P("rec", "tm", None), P("query", None), P(None, "query"), P("rec", "tm"), P("rec"))
    out_specs = (P("rec", "tm", "query"), P("query", "rec"), P(None, "query"))
    return jax.shard_map(
        per_device, mesh=mesh, in_specs=in_specs, out_specs=out_specs, check_vma=False
    )
```

```python
import functools
import math

import jax
import jax.numpy as jnp
from jax import lax
from jax.experimental import pallas as pl
from jax.experimental.pallas import tpu as pltpu
from jax.sharding import PartitionSpec as P


GROUPS = 4
LANES = 128


def spread_taps(kern_ref, lanes):
    taps = kern_ref.shape[0]
    return [jnp.broadcast_to(kern_ref[j : j + 1, lanes], (8, LANES)) for j in range(taps)]


SPAN = 4
AHEAD = 3


def plus(a, b):
    return [x + b[i] if i < len(b) else x for i, x in enumerate(a)]


def minus(a):
    return [-x for x in a]


def spread_filters(filt_ref, h):
    even, odd = h[0::2], h[1::2]
    both = plus(even, odd)
    filters = (
        plus(both[0::2], both[1::2]),
        both[0::2],
        minus(both[1::2]),
        plus(even[0::2], even[1::2]),
        even[0::2],
        minus(even[1::2]),
        minus(plus(odd[0::2], odd[1::2])),
        minus(odd[0::2]),
        odd[1::2],
    )
    depth = len(filters[0])
    for n, one in enumerate(filters):
        for i, x in enumerate(one):
            filt_ref[n * depth + i] = x
    return [len(one) for one in filters]


def spread_streams(load, strm_ref, groups):
    def one_group(g):
        x = [load(pl.multiple_of(g * 32, 32) + o) for o in range(7)]
        e = [x[o] - x[o + 2] for o in range(5)]
        f = [e[o] - e[o + 1] for o in range(4)]
        rows = pl.ds(pl.multiple_of(g * 8, 8), 8)
        streams = (x[3], e[1], e[3], x[2] - x[3], f[0], f[2], x[3] - x[4], f[1], f[3])
        for n, one in enumerate(streams):
            strm_ref[n, rows, :] = one

    def body(i, carry):
        for k in range(AHEAD):
            one_group(i * AHEAD + k)
        return carry

    lax.fori_loop(0, groups // AHEAD, body, 0)
    for g in range(groups // AHEAD * AHEAD, groups):
        one_group(g)


def fir(strm_ref, filt_ref, lengths, base, span):
    depth = lengths[0]
    done = []
    for n, count in enumerate(lengths):
        taps = [filt_ref[n * depth + i] for i in range(count)]
        sums = list(done[n // 3 * 3]) if n % 3 else [None] * span
        for o in range(8 * (span - 1) + count):
            v = strm_ref[n, pl.ds(base + o, 8), :]
            for k in range(span):
                i = o - 8 * k
                if 0 <= i < count:
                    term = taps[i] * v
                    sums[k] = term if sums[k] is None else sums[k] + term
        done.append(sums)
    add = lambda a, b: [x + z for x, z in zip(a, b)]
    return (
        add(done[1], done[4]),
        add(done[1], done[7]),
        add(done[2], done[5]),
        add(done[2], done[8]),
    )


MESH = pl.DeviceIdType.MESH


def bit_reversed(p, bits):
    return sum((p // (1 << k)) % 2 * (1 << (bits - 1 - k)) for k in range(bits))


def gradient_kernel(dims, scale, lab_hbm, len_hbm, fr_hbm, qu_hbm, kern_hbm, *refs):
    tms, peers, recs, chunk, runs, hop, tap_hop = dims
    bits = recs.bit_length() - 1
    gf_ref, gq_ref, gk_ref = refs[:3]
    scratch = refs[3:]
    acc, scratch = scratch[:bits], scratch[bits:]
    arrived, scratch = scratch[:bits], scratch[bits:]
    kacc, scratch = scratch[:bits], scratch[bits:]
    karrived, scratch = scratch[:bits], scratch[bits:]
    (mid, outer, inner, kmid, kouter, kinner, kfin, fpart, fin, sg_ref, grad) = scratch[:11]
    (sc_ref, e_ref, f_ref, lab_ref, valid_ref, xh_ref, hin, hout, stat, stat_in) = scratch[11:21]
    (fr_ref, qu_ref, kern_ref, lab_row, lab_in, len_ref, strm_ref, filt_ref, turn) = scratch[21:30]
    edge_ref, scratch = scratch[30], scratch[31:]
    (rec_send, rec_recv, in_send, out_recv, out_send, inn_recv, f_send, f_recv) = scratch[:8]
    (h_send, h_recv, s_send, s_recv, load_sem, qu_sem) = scratch[8:14]
    (k_send, k_recv, kin_send, kout_recv, kout_send, kinn_recv, kg_send, kg_recv) = scratch[14:]

    t = lax.axis_index("tm")
    y = lax.axis_index("query")
    r = lax.axis_index("rec")
    half = tms // 2
    low = t < half
    is_end = (t == 0) | (t == tms - 1)
    is_mid = (t == half - 1) | (t == half)
    inward = jnp.where(low, t + 1, t - 1)
    outward = jnp.where(low, lax.rem(t + tms - 1, tms), lax.rem(t + 1, tms))
    my_bits = [lax.rem(r // (1 << k), 2) for k in range(bits)]
    rec_peers = [r + (1 - 2 * my_bits[k]) * (1 << k) for k in range(bits)]

    barrier = pltpu.get_barrier_semaphore()

    def greet(device):
        pl.semaphore_signal(barrier, inc=1, device_id=device, device_id_type=MESH)

    for peer in rec_peers:
        greet({"rec": peer})
    for d in range(1, peers):
        greet({"query": lax.rem(y + d, peers)})
    greet({"tm": inward})

    @pl.when(jnp.logical_not(is_end))
    def _():
        greet({"tm": outward})

    edges = [slice(0, 2 * (kern_ref.shape[0] // 2))]
    edges.append(slice(fr_ref.shape[0] - edges[0].stop, fr_ref.shape[0]))
    edge_loads = [
        pltpu.make_async_copy(fr_hbm.at[rows], edge_ref.at[side], load_sem.at[4 + side])
        for side, rows in enumerate(edges)
    ]
    loads = [
        pltpu.make_async_copy(src, dst, load_sem.at[i])
        for i, (src, dst) in enumerate(
            ((fr_hbm, fr_ref), (lab_hbm, lab_row), (len_hbm, len_ref), (kern_hbm, kern_ref))
        )
    ]
    queries, width = qu_ref.shape
    parts = qu_sem.shape[0]
    span = queries // parts

    def qu_load(p):
        rows = pl.ds(p * span, span)
        return pltpu.make_async_copy(qu_hbm.at[rows], qu_ref.at[rows], qu_sem.at[p])

    for one in edge_loads + loads[1:3] + loads[:1]:
        one.start()
    for p in range(parts):
        qu_load(p).start()
    loads[3].start()

    count = queries // chunk
    per = chunk // runs[0][2]
    cols = width // recs
    fcols = width // peers
    row_count = sg_ref.shape[0]
    f_tiles = row_count // LANES
    taps_n = kern_ref.shape[0]
    rim = taps_n // 2
    halo = 2 * rim
    block = 8 * GROUPS
    ext = f_ref.shape[0]
    tiles = e_ref.shape[0]
    wide = valid_ref.shape[0]
    lane = lax.broadcasted_iota(jnp.int32, (8, LANES), 1) + y * queries

    def copy(src, dst, send, recv, device):
        return pltpu.make_async_remote_copy(
            src_ref=src,
            dst_ref=dst,
            send_sem=send,
            recv_sem=recv,
            device_id=device,
            device_id_type=MESH,
        )

    def at(c):
        return pl.ds(pl.multiple_of(c * chunk, chunk), chunk)

    def sub_at(row, size):
        return pl.ds(pl.multiple_of(row, size), size)

    def f_rows(i):
        return pl.ds(pl.multiple_of(i * LANES, LANES), LANES)

    def f_copy(d, i):
        p = lax.rem(y + d, peers)
        return copy(
            fpart.at[p, f_rows(i)],
            fin.at[d - 1, f_rows(i)],
            f_send.at[d - 1, i],
            f_recv.at[d - 1, i],
            {"query": p},
        )

    def f_compute(p, i):
        columns = pl.ds(pl.multiple_of(p * fcols, fcols), fcols)
        fpart[p, f_rows(i), :] = jnp.dot(
            sg_ref[f_rows(i), :], qu_ref[:, columns], preferred_element_type=jnp.float32
        )

    def f_finish():
        for i in range(f_tiles):
            for d in range(1, peers):
                f_copy(d, i).wait_recv()
        total = fpart[y]
        for d in range(1, peers):
            total = total + fin[d - 1]
        gf_ref[...] = (total * scale).astype(gf_ref.dtype)
        for i in range(f_tiles):
            for d in range(1, peers):
                f_copy(d, i).wait_send()

    has = [t > 0, t < tms - 1]

    def halo_copies(side):
        device = {"tm": lax.rem(t + (tms - 1 if side == 0 else 1), tms)}
        return (
            copy(
                hout.at[side],
                hin.at[1 - side],
                h_send.at[0, side],
                h_recv.at[0, 1 - side],
                device,
            ),
            copy(
                lab_row,
                lab_in.at[1 - side],
                h_send.at[1, side],
                h_recv.at[1, 1 - side],
                device,
            ),
        )

    for side in range(2):
        edge_loads[side].wait()
        hout[side] = edge_ref[side].astype(jnp.float32)
    loads[1].wait()
    pl.semaphore_wait(barrier, jnp.where(is_end, bits + peers, bits + peers + 1))

    for side in range(2):
        @pl.when(has[side])
        def _(side=side):
            for one in halo_copies(side):
                one.start()

    loads[2].wait()
    frame = lax.broadcasted_iota(jnp.int32, (wide, LANES), 0) + (t * row_count - halo)
    valid_ref[...] = jnp.where((frame >= 0) & (frame < len_ref[0]), 1.0, 0.0)
    stat[...] = jnp.zeros_like(stat)

    def column_of(row):
        return jnp.transpose(jnp.broadcast_to(row.astype(jnp.float32), (LANES, LANES)))

    for i in range(row_count // LANES):
        lab_ref[rim + i * LANES : rim + (i + 1) * LANES, :] = column_of(
            lab_row[:, i * LANES : (i + 1) * LANES]
        )

    batch = min(BATCH, tiles // parts)

    def score(rows_of, keep):
        def body(c, carry):
            rows = pl.ds(pl.multiple_of(c * batch * LANES, LANES), batch * LANES)
            part = lax.dot_general(
                rows_of[...],
                qu_ref[rows, :],
                (((1,), (1,)), ((), ())),
                preferred_element_type=jnp.float32,
            )
            for h in range(batch):
                for begin, rows in keep:
                    size = rows.stop - rows.start
                    one = part[begin : begin + size, h * LANES : (h + 1) * LANES] * scale
                    one = jnp.where(valid_ref[rows, :] > 0, one, 0.0)
                    sc_ref[batch * c + h, rows, :] = one
            return carry

        return body

    loads[0].wait()
    each = tiles // batch // parts
    own_rows = slice(halo, halo + row_count)
    for p in range(parts):
        qu_load(p).wait()
        lax.fori_loop(p * each, (p + 1) * each, score(fr_ref, [(0, own_rows)]), 0)

    for side in range(2):
        @pl.when(has[side])
        def _(side=side):
            for one in halo_copies(1 - side):
                one.wait_recv()

        @pl.when(jnp.logical_not(has[side]))
        def _(side=side):
            hin[side] = jnp.zeros((halo, width), jnp.float32)
            lab_in[side] = jnp.zeros((1, row_count), jnp.int32)

    xh_ref[:halo, :] = hin[0].astype(jnp.bfloat16)
    xh_ref[halo:, :] = hin[1].astype(jnp.bfloat16)
    lab_ref[:rim, :] = column_of(lab_in[0, :, row_count - LANES :])[LANES - rim :, :]
    lab_ref[rim + row_count :, :] = column_of(lab_in[1, :, :LANES])[:rim, :]

    outer_rows = [(0, slice(0, halo)), (halo, slice(halo + row_count, wide))]
    lax.fori_loop(0, tiles // batch, score(xh_ref, outer_rows), 0)
    loads[3].wait()

    def smoothed(c, carry):
        lengths = spread_filters(filt_ref, spread_taps(kern_ref, at(c)))
        spread_streams(lambda o: sc_ref[c, pl.ds(o, 8, stride=4), :], strm_ref, wide // 32)

        def piece(base, span):
            for p, sums in enumerate(fir(strm_ref, filt_ref, lengths, base, span)):
                for k in range(span):
                    rows = pl.ds(4 * base + 32 * k + p, 8, stride=4)
                    e_ref[c, rows, :] = sums[k]

        def body(g, carry):
            piece(pl.multiple_of(g * 8 * SPAN, 8), SPAN)
            return carry

        whole = ext // (32 * SPAN)
        lax.fori_loop(0, whole, body, 0)
        for g in range(whole * SPAN, ext // 32):
            piece(8 * g, 1)
        return carry

    lax.fori_loop(0, tiles, smoothed, 0)

    diagonal = lax.broadcasted_iota(jnp.int32, (block, LANES), 0) == lax.broadcasted_iota(
        jnp.int32, (block, LANES), 1
    )

    def widest(g, carry):
        rows = pl.ds(pl.multiple_of(g * block, block), block)
        top = e_ref[0, rows, :]
        for c in range(1, tiles):
            top = jnp.maximum(top, e_ref[c, rows, :])
        f_ref[rows, :] = top
        return carry

    lax.fori_loop(0, ext // block, widest, 0)

    def note(i, g, value):
        picked = jnp.where(diagonal, value, 0.0)
        stat[0, i, pl.ds(g, 1), :] = jnp.sum(picked, axis=0, keepdims=True)

    for g in range(ext // block):
        rows = pl.ds(g * block, block)
        top = jnp.max(f_ref[rows, :], axis=1, keepdims=True)
        top = jnp.broadcast_to(top, (block, LANES))
        f_ref[rows, :] = top
        note(0, g, top)

    def exponents(g, carry):
        rows = pl.ds(pl.multiple_of(g * block, block), block)
        top = f_ref[rows, :]
        total = jnp.zeros((block, LANES), jnp.float32)
        for c in range(tiles):
            e = jnp.exp(e_ref[c, rows, :] - top)
            e_ref[c, rows, :] = e
            total = total + e
        f_ref[rows, :] = total
        return carry

    lax.fori_loop(0, ext // block, exponents, 0)

    for g in range(ext // block):
        total = jnp.sum(f_ref[pl.ds(g * block, block), :], axis=1, keepdims=True)
        note(1, g, jnp.broadcast_to(total, (block, LANES)))

    def stat_copy(k):
        bit = lax.rem(y // (1 << k), 2)
        device = {"query": y + (1 - 2 * bit) * (1 << k)}
        return copy(stat.at[k], stat_in.at[k], s_send.at[k], s_recv.at[k], device)

    rounds = peers.bit_length() - 1
    for k in range(rounds):
        stat_copy(k).start()
        stat_copy(k).wait_recv()
        top = jnp.maximum(stat[k, 0], stat_in[k, 0])
        stat[k + 1, 0] = top
        stat[k + 1, 1] = stat[k, 1] * jnp.exp(stat[k, 0] - top) + stat_in[k, 1] * jnp.exp(
            stat_in[k, 0] - top
        )
    stat[rounds, 1] = jnp.exp(stat[0, 0] - stat[rounds, 0]) / stat[rounds, 1]

    for g in range(ext // block):
        rows = pl.ds(g * block, block)
        row = jnp.broadcast_to(stat[rounds, 1, g : g + 1, :], (block, LANES))
        factor = jnp.sum(jnp.where(diagonal, row, 0.0), axis=1, keepdims=True)
        factor = jnp.broadcast_to(factor, (block, LANES))
        valid = valid_ref[pl.ds(g * block + rim, block), :] > 0
        f_ref[rows, :] = jnp.where(valid, factor, -1.0)

    def map_gradient(c):
        first = (lane + c * chunk).astype(jnp.float32)

        def body(g, carry):
            for i in range(GROUPS):
                rows = pl.ds(pl.multiple_of(g * block + 8 * i, 8), 8)
                hit = jnp.where(lab_ref[rows, :] == first, 1.0, 0.0)
                factor = f_ref[rows, :]
                value = e_ref[c, rows, :] * jnp.maximum(factor, 0.0) - hit
                grad[c, rows, :] = jnp.where(factor >= 0.0, value, 0.0)
            return carry

        lax.fori_loop(0, ext // block, body, 0)

    def score_gradient(c):
        lengths = spread_filters(filt_ref, spread_taps(kern_ref, at(c))[::-1])
        spread_streams(lambda o: grad[c, pl.ds(o, 8, stride=4), :], strm_ref, ext // 32)

        def body(g, carry):
            base = pl.multiple_of(g * 8 * SPAN, 8)
            for p, sums in enumerate(fir(strm_ref, filt_ref, lengths, base, SPAN)):
                for k in range(SPAN):
                    turn[pl.ds(32 * k + p, 8, stride=4), :] = sums[k]
            rows = pl.ds(pl.multiple_of(g * 32 * SPAN, 32 * SPAN), 32 * SPAN)
            valid = f_ref[pl.ds(pl.multiple_of(g * 32 * SPAN, 32) + rim, 32 * SPAN), :] >= 0.0
            sg_ref[rows, at(c)] = jnp.where(valid, turn[...], 0.0).astype(jnp.bfloat16)
            return carry

        lax.fori_loop(0, row_count // (32 * SPAN), body, 0)

    def tap_gradient(c):
        def body(g, sums):
            base = pl.multiple_of(g * block, block)
            held = [grad[c, pl.ds(base + rim + 8 * i, 8), :] for i in range(GROUPS)]
            sums = list(sums)
            for o in range(8 * (GROUPS - 1) + taps_n):
                v = sc_ref[c, pl.ds(base + rim + o, 8), :]
                for i in range(GROUPS):
                    j = o - 8 * i
                    if 0 <= j < taps_n:
                        sums[j] = sums[j] + held[i] * v
            return tuple(sums)

        zero = jnp.zeros((8, LANES), jnp.float32)
        sums = lax.fori_loop(0, row_count // block, body, (zero,) * taps_n)
        for j in range(taps_n):
            total = jnp.sum(sums[j], axis=0, keepdims=True)
            kacc[0][c // recs, bit_reversed(c % recs, bits), j : j + 1, :] = total

    def rec_copy(k, m):
        n, rows = recs >> k, sub_at(m[1], m[2])
        theirs = (1 - my_bits[k]) * (n // 2)
        return copy(
            acc[k].at[pl.ds(theirs, n // 2), rows],
            arrived[k].at[:, rows],
            rec_send.at[k, m[0]],
            rec_recv.at[k, m[0]],
            {"rec": rec_peers[k]},
        )

    def summed(k, m):
        rec_copy(k, m).wait_recv()
        n, rows = recs >> k, sub_at(m[1], m[2])
        mine = my_bits[k] * (n // 2)
        return acc[k][pl.ds(mine, n // 2), rows, :] + arrived[k][:, rows, :]

    def inward_copy(m, to_mid):
        rows = sub_at(m[1], m[2])
        big = inner if to_mid else outer
        recv = inn_recv if to_mid else out_recv
        return copy(mid.at[rows], big.at[rows], in_send.at[m[0]], recv.at[m[0]], {"tm": inward})

    def outward_copy(m):
        rows = sub_at(m[1], m[2])
        return copy(
            inner.at[rows], inner.at[rows], out_send.at[m[0]], inn_recv.at[m[0]], {"tm": outward}
        )

    def produce(c):
        map_gradient(c)
        score_gradient(c)
        part = lax.dot_general(
            sg_ref[:, at(c)],
            fr_ref[...],
            (((0,), (0,)), ((), ())),
            preferred_element_type=jnp.float32,
        )
        for p in range(recs):
            j = bit_reversed(p, bits)
            acc[0][p, at(c), :] = part[:, j * cols : (j + 1) * cols]

        @pl.when(c < count - 1)
        def _():
            for h in range(per):
                first = c * per + h
                rec_copy(0, (first, first * runs[0][2], runs[0][2])).start()

        @pl.when(c == count - 1)
        def _():
            for index, row, size, number in runs:
                for h in range(number):
                    if row + h * size >= queries - chunk:
                        rec_copy(0, (index + h, row + h * size, size)).start()

    def exchange(k, m):
        acc[k][:, sub_at(m[1], m[2]), :] = summed(k - 1, m)
        rec_copy(k, m).start()

    def gather_in(m):
        rows = sub_at(m[1], m[2])
        mid[rows, :] = summed(bits - 1, m)[0]

        @pl.when(jnp.logical_not(is_end))
        def _():
            inward_copy(m, False).wait_recv()
            mid[rows, :] += outer[rows, :]

        @pl.when(is_mid)
        def _():
            inward_copy(m, True).start()

        @pl.when(jnp.logical_not(is_mid))
        def _():
            inward_copy(m, False).start()

    def spread_out(m):
        rows = sub_at(m[1], m[2])
        inward_copy(m, True).wait_recv()

        @pl.when(is_mid)
        def _():
            inner[rows, :] += mid[rows, :]

        @pl.when(jnp.logical_not(is_end))
        def _():
            outward_copy(m).start()

        gq_ref[rows, :] = (inner[rows, :] * scale).astype(gq_ref.dtype)
        for k in range(bits):
            rec_copy(k, m).wait_send()
        inward_copy(m, False).wait_send()

    def k_copy(k, i):
        n = recs >> k
        theirs = (1 - my_bits[k]) * (n // 2)
        return copy(
            kacc[k].at[i, pl.ds(theirs, n // 2)],
            karrived[k].at[i],
            k_send.at[k, i],
            k_recv.at[k, i],
            {"rec": rec_peers[k]},
        )

    def k_summed(k, i):
        k_copy(k, i).wait_recv()
        n = recs >> k
        return kacc[k][i, pl.ds(my_bits[k] * (n // 2), n // 2)] + karrived[k][i]

    def k_inward(i, to_mid):
        dst = kinner if to_mid else kouter
        recv = kinn_recv if to_mid else kout_recv
        return copy(kmid.at[i], dst.at[i], kin_send.at[i], recv.at[i], {"tm": inward})

    def k_outward(i):
        return copy(kinner.at[i], kinner.at[i], kout_send.at[i], kinn_recv.at[i], {"tm": outward})

    place = sum(my_bits[k] * (recs >> (k + 1)) for k in range(bits))

    def k_give(k, i):
        n = recs >> (k + 1)
        rows = pl.ds(place // n * n, n)
        return copy(
            kfin.at[i, rows],
            kfin.at[i, rows],
            kg_send.at[k, i],
            kg_recv.at[k, i],
            {"rec": rec_peers[k]},
        )

    def k_exchange(k, i):
        kacc[k][i] = k_summed(k - 1, i)
        k_copy(k, i).start()

    def k_gather(i):
        kmid[i] = k_summed(bits - 1, i)[0]

        @pl.when(jnp.logical_not(is_end))
        def _():
            k_inward(i, False).wait_recv()
            kmid[i] += kouter[i]

        @pl.when(is_mid)
        def _():
            k_inward(i, True).start()

        @pl.when(jnp.logical_not(is_mid))
        def _():
            k_inward(i, False).start()

    def k_spread(i):
        k_inward(i, True).wait_recv()

        @pl.when(is_mid)
        def _():
            kinner[i] += kmid[i]

        @pl.when(jnp.logical_not(is_end))
        def _():
            k_outward(i).start()

        kfin[i, place] = kinner[i]
        k_give(bits - 1, i).start()
        for k in range(bits):
            k_copy(k, i).wait_send()
        k_inward(i, False).wait_send()

    def k_take(k, i):
        k_give(k, i).wait_recv()
        if k > 0:
            k_give(k - 1, i).start()
        else:
            for p in range(recs):
                gk_ref[:, at(i * recs + p)] = kfin[i, bit_reversed(p, bits)]

    reach = half - 1
    away = jnp.where(low, reach - t, t - half)

    def plan(step, first, spread, gather, swap, take):
        base = first + (bits - 1) * step
        ends = base + 2 * step * reach + step
        late = [
            (ends + (bits - 1 - k) * step + (step if k else first), functools.partial(take, k))
            for k in range(bits if take else 0)
        ]
        late += [(base + step * (reach + away + 1), spread), (base + step * (reach - away), gather)]
        late += [
            (first + (k - 1) * step, functools.partial(swap, k)) for k in range(bits - 1, 0, -1)
        ]
        return late, ends + ((bits - 1) * step + first if take else 0)

    stages, last = plan(hop, 1, spread_out, gather_in, exchange, None)
    k_stages, k_last = plan(tap_hop, 1, k_spread, k_gather, k_exchange, k_take)
    begun = 2 * count
    quads = count // recs
    made = lambda c: c + 1 + max(c + 1 - f_tiles, 0) // 2
    gap = next(
        x for x in range(1, recs + 1) if all(made(x * q) >= recs * q for q in range(1, quads + 1))
    )
    k_stages = k_stages + [(0, lambda i: k_copy(0, i).start())]
    f_own = max(begun, count + (peers - 1) * f_tiles)
    f_end = f_own + f_tiles
    messages = runs[-1][0] + runs[-1][3]
    steps = max(messages + last, count + 1 + gap * quads + k_last, f_end + 1)

    def step(s, carry):
        @pl.when(s < count)
        def _():
            produce(s)

        c = s - count

        @pl.when((c >= 0) & (c < (peers - 1) * f_tiles))
        def _():
            i = c % f_tiles
            f_compute(lax.rem(y + 1 + c // f_tiles, peers), i)

            for d in range(1, peers):
                @pl.when(c // f_tiles == d - 1)
                def _(d=d):
                    f_copy(d, i).start()

        @pl.when((s >= f_own) & (s < f_own + f_tiles))
        def _():
            f_compute(y, s - f_own)

        @pl.when(s == f_end)
        def _():
            f_finish()

        @pl.when((c >= 0) & (c < count))
        def _():
            def tap(i, carry):
                tap_gradient(i)
                return carry

            begin = c + jnp.maximum(c - f_tiles, 0) // 2
            end = c + 1 + jnp.maximum(c + 1 - f_tiles, 0) // 2
            lax.fori_loop(jnp.minimum(begin, count), jnp.minimum(end, count), tap, 0)

        for delay, stage in stages:
            for index, row, size, number in runs:
                tick = s - delay - index

                @pl.when((tick >= 0) & (tick < number))
                def _(stage=stage, tick=tick, index=index, row=row, size=size):
                    stage((index + tick, row + tick * size, size))

        for delay, stage in k_stages:
            tick = c - delay

            @pl.when((tick >= gap) & (tick <= gap * quads) & (lax.rem(tick + gap * steps, gap) == 0))
            def _(stage=stage, tick=tick):
                stage(tick // gap - 1)

        return carry

    lax.fori_loop(0, steps, step, 0)

    @pl.when(jnp.logical_not(is_end))
    def _():
        for index, row, size, number in runs:
            def drain(h, carry, index=index, row=row, size=size):
                outward_copy((index + h, row + h * size, size)).wait_send()
                return carry

            lax.fori_loop(0, number, drain, 0)

    def k_drain(i, carry):
        for k in range(bits):
            k_give(k, i).wait_send()

        @pl.when(jnp.logical_not(is_end))
        def _():
            k_outward(i).wait_send()

        return carry

    lax.fori_loop(0, count // recs, k_drain, 0)
    for k in range(rounds):
        stat_copy(k).wait_send()
    for side in range(2):
        @pl.when(has[side])
        def _(side=side):
            for one in halo_copies(side):
                one.wait_send()


PIECE = 64
TAIL = (64, 64)


def message_runs(queries):
    runs, row, index = [], 0, 0
    body = (queries - sum(TAIL)) // PIECE
    for size, number in [(PIECE, body)] + [(size, 1) for size in TAIL]:
        if runs and runs[-1][2] == size:
            runs[-1] = runs[-1][:3] + (runs[-1][3] + number,)
        else:
            runs.append((index, row, size, number))
        index, row = index + number, row + size * number
    return tuple(runs)


HOP = 3
TAP_HOP = 3
PARTS = 2
BATCH = 4


def gradients(labels, lengths, frame_rows, queries, kernel, scale):
    tms, peers, recs = (lax.axis_size("tm"), lax.axis_size("query"), lax.axis_size("rec"))
    bits = recs.bit_length() - 1
    row_count, width = frame_rows.shape
    query_count = queries.shape[0]
    taps = kernel.shape[0]
    chunk = LANES
    runs = message_runs(query_count)
    messages = runs[-1][0] + runs[-1][3]
    count = query_count // chunk
    cols, fcols = (width // recs, width // peers)
    rim = taps // 2
    ext, wide = (row_count + 2 * rim, row_count + 4 * rim)
    rounds = peers.bit_length() - 1
    stat_rows = (ext // (8 * GROUPS) + 7) // 8 * 8
    quads = count // recs
    f32 = jnp.float32
    vmem = pltpu.VMEM
    small = vmem((quads, taps, chunk), f32)
    block = vmem((query_count, cols), f32)
    scratch = [vmem((recs >> k, query_count, cols), f32) for k in range(bits)]
    scratch += [vmem((recs >> (k + 1), query_count, cols), f32) for k in range(bits)]
    scratch += [vmem((quads, recs >> k, taps, chunk), f32) for k in range(bits)]
    scratch += [vmem((quads, recs >> (k + 1), taps, chunk), f32) for k in range(bits)]
    scratch += [block] * 3 + [small] * 3 + [vmem((quads, recs, taps, chunk), f32)]
    scratch += [
        vmem((peers, row_count, fcols), f32),
        vmem((peers - 1, row_count, fcols), f32),
        vmem((row_count, query_count), jnp.bfloat16),
        vmem((count, ext + 8, chunk), f32),
        vmem((count, wide + 8, chunk), f32),
        vmem((count, ext, chunk), f32),
        vmem((ext, chunk), f32),
        vmem((ext, chunk), f32),
        vmem((wide, chunk), f32),
        vmem((4 * rim, width), jnp.bfloat16),
        vmem((2, 2 * rim, width), f32),
        vmem((2, 2 * rim, width), f32),
        vmem((rounds + 1, 2, stat_rows, LANES), f32),
        vmem((rounds, 2, stat_rows, LANES), f32),
        vmem((row_count, width), jnp.bfloat16),
        vmem((query_count, width), jnp.bfloat16),
        vmem((taps, query_count), f32),
        vmem((1, row_count), jnp.int32),
        vmem((2, 1, row_count), jnp.int32),
        pltpu.SMEM((1,), jnp.int32),
        vmem((9, wide // 4, chunk), f32),
        vmem((9 * (taps // 4 + 1), 8, chunk), f32),
        vmem((32 * SPAN, chunk), f32),
        vmem((2, 2 * rim, width), jnp.bfloat16),
    ]
    dma = pltpu.SemaphoreType.DMA
    scratch += [dma((bits, messages))] * 2 + [dma((messages,))] * 4 + [dma((peers - 1, row_count // LANES))] * 2
    scratch += [dma((2, 2))] * 2 + [dma((rounds,))] * 2 + [dma((6,)), dma((PARTS,))]
    scratch += [dma((bits, quads))] * 2 + [dma((quads,))] * 4 + [dma((bits, quads))] * 2
    hbm = pl.BlockSpec(memory_space=pl.ANY)
    dims = (tms, peers, recs, chunk, runs, HOP, TAP_HOP)
    return pl.pallas_call(
        functools.partial(gradient_kernel, dims, scale),
        out_shape=(
            pltpu.VMEM((row_count, fcols), jnp.bfloat16),
            pltpu.VMEM((query_count, cols), jnp.bfloat16),
            pltpu.VMEM((taps, query_count), f32),
        ),
        in_specs=[hbm] * 5,
        out_specs=(pl.BlockSpec(memory_space=pltpu.VMEM),) * 3,
        scratch_shapes=scratch,
        compiler_params=pltpu.CompilerParams(
            collective_id=0, has_side_effects=True, vmem_limit_bytes=60 * 1024 * 1024
        ),
        name="gradients",
    )(labels, lengths, frame_rows, queries, kernel)


def store_kernel(*refs):
    ins, outs, sem = refs[:3], refs[3:6], refs[6]
    copies = [pltpu.make_async_copy(a, b, sem.at[i]) for i, (a, b) in enumerate(zip(ins, outs))]
    for one in copies:
        one.start()
    for one in copies:
        one.wait()


def store(arrays):
    return pl.pallas_call(
        store_kernel,
        out_shape=tuple(jax.ShapeDtypeStruct(a.shape, a.dtype) for a in arrays),
        in_specs=[pl.BlockSpec(memory_space=pltpu.VMEM)] * 3,
        out_specs=(pl.BlockSpec(memory_space=pl.ANY),) * 3,
        scratch_shapes=[pltpu.SemaphoreType.DMA((3,))],
        compiler_params=pltpu.CompilerParams(vmem_limit_bytes=4 * 1024 * 1024),
        name="store",
    )(*arrays)


def per_device(frames, queries, kernel, labels, lengths):
    frame_rows = frames[0]
    width = frame_rows.shape[1]
    logit_scale = 10.0 / math.sqrt(width)
    grad_frames, grad_queries, grad_kernel = store(
        gradients(labels, lengths, frame_rows, queries, kernel, logit_scale)
    )
    return (grad_frames[None], grad_queries, grad_kernel)


def solution(mesh):
    in_specs = (P("rec", "tm", None), P("query", None), P(None, "query"), P("rec", "tm"), P("rec"))
    out_specs = (P("rec", "tm", "query"), P("query", "rec"), P(None, "query"))
    return jax.shard_map(
        per_device, mesh=mesh, in_specs=in_specs, out_specs=out_specs, check_vma=False
    )
```
